256 devices in a mesh: seg: 32 (over y, x, core), fsdp: 8 (over z).
Axes of the slice: x: 4, y: 4, z: 8, core: 2. Of those that a mesh axis runs over, the one named last changes fastest.
Arguments:
- tokens: bfloat16 [8, 8192, 4096], P('fsdp', 'seg')
- w_query: bfloat16 [4096, 2048], P(('seg', 'fsdp'))
- w_key: bfloat16 [4096, 512], P(('seg', 'fsdp'))
- value_weight: bfloat16 [4096, 512], P(('seg', 'fsdp')), may hold values from -0.09375 to 0.09375
- gate_bias: float32 [16], replicated, may hold values from -2 to 2
- block_mask: int32 [8, 32, 2, 2], P('fsdp', 'seg'), may hold values from 0 to 1, as said below
- valid_len: int32 [8, 32], P('fsdp', 'seg'), may hold values from 1 to 256, as said below
Outputs:
- attended: bfloat16 [8, 8192, 2048], P('fsdp', 'seg')
The draws below stay inside these ranges and needn't reach their ends.
Inputs may be any that keep to these rules, and one draw needn't show every extreme that they name: block_mask[b, s] is 1 on its diagonal, 0 above it, and 0 or 1 below it. `valid_len`: the first segment of every book is full.
All inputs are finite; a program needn't handle non-finite values.
Results may differ from the reference program's by a relative error of at most 0.0095.
Values may be sent and summed in bfloat16 or wider, within the bound.
A program may use at most 128 MiB of HBM per device.

```python
import jax
import jax.numpy as jnp
from jax import lax

MODEL_WIDTH = 4096
HEAD_SIZE = 128
QUERY_HEADS = 16
KEY_VALUE_HEADS = 4
BLK = 128
SEG_LEN = 256
NB = 2
SEGS = 32
BOOKS = 8


def query_weight_matrix(key):
    return jax.random.normal(jax.random.fold_in(key, 11), (MODEL_WIDTH, QUERY_HEADS * HEAD_SIZE), jnp.float32) * MODEL_WIDTH ** (-0.5)


def draw_w_query(key, part):
    return query_weight_matrix(key).astype(jnp.bfloat16)


def draw_w_key(key, part):
    own_part = jax.random.normal(jax.random.fold_in(key, 12), (MODEL_WIDTH, KEY_VALUE_HEADS * HEAD_SIZE), jnp.float32) * MODEL_WIDTH ** (-0.5)
    result = own_part
    return result.astype(jnp.bfloat16)


def draw_tokens(key, part):
    length = SEGS * SEG_LEN
    offset = jax.random.normal(jax.random.fold_in(key, 21), (BOOKS, SEGS, 1, MODEL_WIDTH), jnp.float32) * 1.5
    offset = jnp.broadcast_to(offset, (BOOKS, SEGS, SEG_LEN, MODEL_WIDTH)).reshape(BOOKS, length, MODEL_WIDTH)
    noise = jax.random.normal(jax.random.fold_in(key, 22), (BOOKS, length, MODEL_WIDTH), jnp.float32)
    result = noise + offset
    return result.astype(jnp.bfloat16)


def draw_block_mask(key, part):
    bits = jax.random.randint(jax.random.fold_in(key, 31), (BOOKS, SEGS, NB, NB), 0, 2, jnp.int32)
    rows = jnp.arange(NB, dtype=jnp.int32)[:, None]
    cols = jnp.arange(NB, dtype=jnp.int32)[None, :]
    return jnp.where(rows == cols, 1, jnp.where(cols < rows, bits, 0)).astype(jnp.int32)


def draw_valid_len(key, part):
    pick = jax.random.randint(jax.random.fold_in(key, 41), (BOOKS, SEGS), 0, 4, jnp.int32)
    short = jax.random.randint(jax.random.fold_in(key, 42), (BOOKS, SEGS), 1, SEG_LEN + 1, jnp.int32)
    lengths = jnp.where(pick > 0, SEG_LEN, short)
    first = jnp.arange(SEGS, dtype=jnp.int32)[None, :] == 0
    return jnp.where(first, SEG_LEN, lengths).astype(jnp.int32)


def steps_of(rng, extent, shards, low, top_value):
    factor_of, own = 1.0, jax.random.fold_in(rng, 6)
    for position, parts in shards:
        heights = jnp.exp(jax.random.uniform(jax.random.fold_in(own, position), (parts,), jnp.float32, low / len(shards), top_value / len(shards)))
        factor_of = factor_of * jnp.repeat(heights, extent[position] // parts).reshape([-1 if axis == position else 1 for axis in range(len(extent))])
    return factor_of


def bell_draw(own_key, shape, scale, most, pieces=(), kind=jnp.bfloat16):
    values = scale * jax.random.normal(own_key, shape, jnp.float32)
    if pieces:
        values = values * steps_of(own_key, shape, pieces, -0.22, 0.18)
    return jnp.clip(values, -most, most).astype(kind)


def setup_inputs(seed: int = 0) -> dict:
    arg_keys = jax.random.split(jax.random.key(seed), 8)
    tokens = draw_tokens(jax.random.fold_in(arg_keys[7], 71), 0)
    w_query = draw_w_query(jax.random.fold_in(arg_keys[7], 71), 0)
    w_key = draw_w_key(jax.random.fold_in(arg_keys[7], 71), 0)
    value_weight = bell_draw(arg_keys[3], (MODEL_WIDTH, KEY_VALUE_HEADS * HEAD_SIZE), MODEL_WIDTH ** -0.5, 0.09375, ((0, 256),))
    gate_bias = jnp.clip(jax.random.uniform(arg_keys[4], (QUERY_HEADS,), jnp.float32, -2.0, 2.0), -2.0, 2.0)
    block_mask = draw_block_mask(jax.random.fold_in(arg_keys[7], 71), 0)
    valid_len = draw_valid_len(jax.random.fold_in(arg_keys[7], 71), 0)
    return dict(tokens=tokens, w_query=w_query, w_key=w_key, value_weight=value_weight, gate_bias=gate_bias, block_mask=block_mask, valid_len=valid_len)


def sigma_plus(v):
    return jax.nn.elu(v) + 1.0


def segment_delta(keys, values, valid):
    length = keys.shape[0]
    heads_kv = keys.shape[1] // HEAD_SIZE
    live = (jnp.arange(length, dtype=jnp.int32) < valid)[:, None, None]
    sig_keys = jnp.where(live, sigma_plus(keys.reshape(length, heads_kv, HEAD_SIZE).astype(jnp.float32)), 0.0)
    delta_m = jnp.einsum("jgd,jge->gde", sig_keys, values.reshape(length, heads_kv, HEAD_SIZE).astype(jnp.float32), precision=lax.Precision.HIGHEST)
    delta_z = jnp.sum(sig_keys, axis=0)
    return delta_m, delta_z


def segment_output(queries, keys, values, gate_bias, mask_blocks, valid, memory, normalizer):
    length = queries.shape[0]
    heads_kv = memory.shape[0]
    group = queries.shape[1] // (heads_kv * HEAD_SIZE)
    nblocks = mask_blocks.shape[0]
    q_heads = queries.reshape(length, heads_kv, group, HEAD_SIZE)
    k_heads = keys.reshape(length, heads_kv, HEAD_SIZE)
    v_heads = values.reshape(length, heads_kv, HEAD_SIZE)
    scores = jnp.einsum("igxd,jgd->gxij", q_heads.astype(jnp.float32), k_heads.astype(jnp.float32), precision=lax.Precision.HIGHEST) * (HEAD_SIZE ** -0.5)
    full = jnp.broadcast_to(mask_blocks[:, None, :, None], (nblocks, BLK, nblocks, BLK)).reshape(length, length)
    pos = jnp.arange(length, dtype=jnp.int32)
    allowed = (full > 0) & (pos[None, :] <= pos[:, None]) & (pos[None, :] < valid)
    masked = jnp.where(allowed, scores, -1e30)
    top = jnp.max(masked, axis=-1, keepdims=True)
    expo = jnp.where(allowed, jnp.exp(masked - top), 0.0)
    total = jnp.maximum(jnp.sum(expo, axis=-1, keepdims=True), 1.0)
    weights = (expo / total).astype(jnp.bfloat16)
    local = jnp.einsum("gxij,jgd->igxd", weights.astype(jnp.float32), v_heads.astype(jnp.float32), precision=lax.Precision.HIGHEST)
    sig_q = sigma_plus(q_heads.astype(jnp.float32))
    numer = jnp.einsum("igxd,gde->igxe", sig_q, memory, precision=lax.Precision.HIGHEST)
    denom = jnp.einsum("igxd,gd->igx", sig_q, normalizer, precision=lax.Precision.HIGHEST) + 1.0
    gate = jax.nn.sigmoid(gate_bias).reshape(heads_kv, group)[None, :, :, None]
    mixed = gate * (numer / denom[..., None]) + (1.0 - gate) * local
    live = (pos < valid)[:, None, None, None]
    return jnp.where(live, mixed, 0.0).reshape(length, -1).astype(jnp.bfloat16)


def reference(tokens, w_query, w_key, value_weight, gate_bias, block_mask, valid_len):
    heads_kv = w_key.shape[1] // HEAD_SIZE

    def one_book(book):
        book_tokens, book_masks, book_valid = book
        segs = book_tokens.reshape(SEGS, SEG_LEN, MODEL_WIDTH)

        def step(carry, item):
            memory, normalizer = carry
            seg_tokens, mask_blocks, valid = item
            queries = jnp.dot(seg_tokens, w_query, preferred_element_type=jnp.float32).astype(jnp.bfloat16)
            keys = jnp.dot(seg_tokens, w_key, preferred_element_type=jnp.float32).astype(jnp.bfloat16)
            values = jnp.dot(seg_tokens, value_weight, preferred_element_type=jnp.float32).astype(jnp.bfloat16)
            output = segment_output(queries, keys, values, gate_bias, mask_blocks, valid, memory, normalizer)
            delta_m, delta_z = segment_delta(keys, values, valid)
            return (memory + delta_m, normalizer + delta_z), output

        start = (jnp.zeros((heads_kv, HEAD_SIZE, HEAD_SIZE), jnp.float32), jnp.zeros((heads_kv, HEAD_SIZE), jnp.float32))
        carry, outputs = lax.scan(step, start, (segs, book_masks, book_valid))
        return outputs.reshape(SEGS * SEG_LEN, -1)

    return lax.map(one_book, (tokens, block_mask, valid_len))
```

```python
import functools

import jax
import jax.numpy as jnp
from jax import lax
from jax.experimental import pallas as pl
from jax.experimental.pallas import tpu as pltpu
from jax.sharding import PartitionSpec as P

HEAD = 128
SEG = 256
CW = 256
NCH = 6
ORDERS = (("x", "y", "z"), ("y", "z", "x"), ("z", "x", "y"))
MESH_ID = pl.DeviceIdType.MESH
F32 = jnp.float32
BF16 = jnp.bfloat16

PROGRAM = (
    [(c, 0) for c in (0, 1, 2)]
    + [(c, 1) for c in (0, 1, 2)]
    + [(c, 2) for c in (0, 1, 2)]
    + [(2, 3), (0, 3), (1, 3), (2, 4), (0, 4), (1, 4)]
    + [(c, 0) for c in (3, 4, 5)]
    + [(2, 5), (1, 5)]
    + [(c, 1) for c in (3, 4, 5)]
    + [(2, 6), (1, 6)]
    + [(c, 2) for c in (3, 4, 5)]
    + [(0, 5)]
    + [(5, 3), (4, 3), (3, 3), (5, 4), (4, 4), (5, 5), (4, 5)]
    + [(0, 6), (2, 7), (5, 6), (1, 7), (4, 6), (0, 7), (3, 4), (0, 8)]
    + ["keys", (1, 8), "values", "delta", (2, 8), (3, 5), "q0", (3, 6), "rows"]
    + [(4, 7), (5, 7), (3, 7), "memory", "a0", (3, 8), "q1", "a1", (4, 8), "q2", "a2", (5, 8), "q3", "a3"]
)


def sigma(v):
    return jnp.where(v > 0, v, jnp.exp(jnp.minimum(v, 0.0)) - 1.0) + 1.0


def body(
    dims,
    tok_hbm, wq_hbm, wk_hbm, wv_hbm, gate_ref, mask_ref, valid_ref,
    out_hbm,
    w, tok, acc, kbuf, vbuf, qbuf, meta, own, rx, ry, mem, stage,
    recv, send, csem_l, csem_s, csem_r, dsem_s, dsem_r, osem_l, osem_s, osem_r,
):
    seg = lax.axis_index("seg")
    z = lax.axis_index("fsdp")
    c = lax.rem(seg, 2)
    x = lax.rem(seg // 2, dims["x"])
    y = seg // (2 * dims["x"])
    pos = {"x": x, "y": y, "z": z}

    def device(xx, yy, cc, zz):
        return {"seg": (yy * dims["x"] + xx) * 2 + cc, "fsdp": zz}

    def shifted(dim, delta):
        at = dict(pos)
        at[dim] = lax.rem(pos[dim] + delta + dims[dim], dims[dim])
        return device(at["x"], at["y"], c, at["z"])

    sibling = device(x, y, 1 - c, z)

    barrier = pltpu.get_barrier_semaphore()
    peers = [sibling, shifted("z", 1), shifted("z", -1)]
    for dim in "xy":
        peers += [shifted(dim, k) for k in range(1, dims[dim])]
    for peer in peers:
        pl.semaphore_signal(barrier, inc=1, device_id=peer, device_id_type=MESH_ID)
    pl.semaphore_wait(barrier, len(peers))

    locals_, sends_, recvs_ = [], [], []

    def columns(ch, core):
        if ch < 2:
            return (wk_hbm, wv_hbm)[ch].at[:, pl.ds(pl.multiple_of(core * CW, CW), CW)]
        return wq_hbm.at[:, pl.ds(pl.multiple_of(core * 4 * CW + (ch - 2) * CW, CW), CW)]

    for ch in range(NCH):
        slot = w.at[ch, y, x, c, z]
        other = w.at[ch, y, x, 1 - c, z]
        there = pltpu.make_async_remote_copy(
            columns(ch, 1 - c), slot, csem_s.at[ch], csem_r.at[ch], device_id=sibling, device_id_type=MESH_ID
        )
        there.start()
        here = pltpu.make_async_copy(columns(ch, c), slot, csem_l.at[ch])
        here.start()
        back = pltpu.make_async_remote_copy(
            other, other, csem_s.at[ch], csem_r.at[ch], device_id=sibling, device_id_type=MESH_ID
        )
        locals_.append(here)
        sends_.append(there)
        recvs_.append(back)

    row8 = lax.broadcasted_iota(jnp.int32, (8, HEAD), 0)
    meta[c] = jnp.where(row8 == 0, valid_ref[0, 0], mask_ref[1, 0])
    meta_copy = pltpu.make_async_remote_copy(
        meta.at[c], meta.at[c], csem_s.at[NCH], csem_r.at[NCH], device_id=sibling, device_id_type=MESH_ID
    )
    meta_back = pltpu.make_async_remote_copy(
        meta.at[1 - c], meta.at[1 - c], csem_s.at[NCH], csem_r.at[NCH], device_id=sibling, device_id_type=MESH_ID
    )
    tok_copy = pltpu.make_async_remote_copy(
        tok_hbm, tok.at[c], csem_s.at[NCH + 1], csem_r.at[NCH + 1], device_id=sibling, device_id_type=MESH_ID
    )
    tok_back = pltpu.make_async_remote_copy(
        tok.at[1 - c], tok.at[1 - c], csem_s.at[NCH + 1], csem_r.at[NCH + 1], device_id=sibling, device_id_type=MESH_ID
    )
    tok_here = pltpu.make_async_copy(tok_hbm, tok.at[c], csem_l.at[NCH])

    def block(ch, order, stage_no, index, half):
        cols = slice(None) if half is None else pl.ds(half * (CW // 2), CW // 2)
        at = {d: pl.ds(pos[d], 1) for d in "xyz"}
        for d in order[:stage_no]:
            at[d] = slice(None)
        at[order[stage_no]] = pl.ds(index, 1)
        return w.at[ch, at["y"], at["x"], :, at["z"], :, cols]

    steps = {}
    for ch in range(NCH):
        order = ORDERS[ch % 3]
        steps[ch] = [(s, k) for s in range(3) for k in range(1, dims[order[s]] // 2 + 1)]

    def ring(ch, number, arriving):
        order = ORDERS[ch % 3]
        s, k = steps[ch][number]
        dim = order[s]
        n = dims[dim]
        copies = []
        for side, delta in ((0, 1), (1, -1)):
            back = k if arriving else k - 1
            index = lax.rem(pos[dim] - delta * back + n, n)
            half = side if 2 * k == n else None
            piece = block(ch, order, s, index, half)
            copies.append(
                pltpu.make_async_remote_copy(
                    piece, piece, send.at[ch, number, side], recv.at[ch, number, side],
                    device_id=shifted(dim, delta), device_id_type=MESH_ID,
                )
            )
        return copies

    sent = []

    def tick(ch, number):
        arrived = ring(ch, number - 1, True) if number else None
        leaving = ring(ch, number, False) if number < len(steps[ch]) else None
        if number == 0:
            locals_[ch].wait()
            recvs_[ch].wait_recv()
        same_stage = leaving is not None and number and steps[ch][number][0] == steps[ch][number - 1][0]
        if same_stage:
            for a, b in zip(arrived, leaving):
                a.wait_recv()
                b.start()
        else:
            if arrived is not None:
                for a in arrived:
                    a.wait_recv()
            if leaving is not None:
                for b in leaving:
                    b.start()
        if leaving is not None:
            sent.extend(leaving)

    def project(ch, dst):
        def part(i, first):
            a = tok[:, :, pl.ds(pl.multiple_of(i * 1024, 1024), 1024)].reshape(2 * SEG, 1024)
            b = w[ch, i].reshape(1024, CW)
            r = jnp.dot(a, b, preferred_element_type=F32)
            if first:
                acc[...] = r
            else:
                acc[...] += r

        part(0, True)

        @pl.loop(1, dims["y"])
        def _(i):
            part(i, False)

        dst[...] = acc[...].astype(BF16).reshape(2, SEG, CW)

    def delta():
        jrow = lax.broadcasted_iota(jnp.int32, (SEG, HEAD), 0)
        for g in range(2):
            cols = slice(g * HEAD, (g + 1) * HEAD)
            both = []
            for s in range(2):
                live = jrow < meta[s, 0:1, :]
                sig = jnp.where(live, sigma(kbuf[s, :, cols].astype(F32)), 0.0)
                zrow = jnp.sum(sig, axis=0, keepdims=True)
                m = lax.dot_general(
                    sig.astype(BF16), vbuf[s, :, cols], (((0,), (0,)), ((), ())), preferred_element_type=F32
                )
                both.append((m, zrow))
            own[g, 0:HEAD, :] = both[0][0]
            own[g, HEAD : HEAD + 16, :] = jnp.broadcast_to(both[0][1], (16, HEAD))
            rx[x, g, 0:HEAD, :] = (both[0][0] + both[1][0]).astype(BF16)
            rx[x, g, HEAD : HEAD + 16, :] = jnp.broadcast_to(both[0][1] + both[1][1], (16, HEAD)).astype(BF16)

    def exchange(dim, buf, number, arriving):
        n = dims[dim]
        copies = []
        for k in range(1, n):
            index = lax.rem(pos[dim] - k + n, n) if arriving else pos[dim]
            copies.append(
                pltpu.make_async_remote_copy(
                    buf.at[index], buf.at[index], dsem_s.at[number, k - 1], dsem_r.at[number, k - 1],
                    device_id=shifted(dim, k), device_id_type=MESH_ID,
                )
            )
        return copies

    def launch(copies):
        for one in copies:
            one.start()
        sent.extend(copies)

    def row_totals():
        for one in exchange("x", rx, 0, True):
            one.wait_recv()
        for g in range(2):
            total = jnp.zeros((HEAD + 16, HEAD), F32)
            for k in range(dims["x"]):
                total = total + rx[k, g].astype(F32)
            ry[y, g] = total.astype(BF16)
        launch(exchange("y", ry, 1, False))

    def memory():
        for one in exchange("y", ry, 1, True):
            one.wait_recv()
        for g in range(2):
            total = jnp.zeros((HEAD + 16, HEAD), F32)
            for k in range(dims["x"]):
                total = total + jnp.where(k < x, rx[k, g].astype(F32), 0.0)
            for k in range(dims["y"]):
                total = total + jnp.where(k < y, ry[k, g].astype(F32), 0.0)
            for s in range(2):
                if s:
                    total = total + own[g]
                mem[s, g, :, 0:HEAD] = total[0:HEAD].astype(BF16)
                zcol = jnp.transpose(jnp.broadcast_to(total[HEAD : HEAD + 1], (HEAD, HEAD)))
                mem[s, g, :, HEAD:] = zcol.astype(BF16)

    ones = jnp.ones((SEG, HEAD), BF16)

    def attend(j):
        g = j // 2
        kcols = slice(g * HEAD, (g + 1) * HEAD)
        gates = []
        for e in range(2):
            bias = jnp.full((1, HEAD), gate_ref[c * 8 + 2 * j + e], F32)
            gates.append(jax.nn.sigmoid(bias))
        for s in range(2):
            valid = meta[s, 0:1, :]
            for r in range(2):
                nk = (r + 1) * HEAD
                rows = slice(r * HEAD, (r + 1) * HEAD)
                q = jnp.concatenate([qbuf[j, s, rows, 0:HEAD], qbuf[j, s, rows, HEAD:]], axis=0)
                keys = kbuf[s, 0:nk, kcols]
                vals = jnp.concatenate([vbuf[s, 0:nk, kcols], ones[0:nk]], axis=1)
                scores = lax.dot_general(q, keys, (((1,), (1,)), ((), ())), preferred_element_type=F32)
                irow = lax.broadcasted_iota(jnp.int32, (HEAD, nk), 0) + r * HEAD
                jcol = lax.broadcasted_iota(jnp.int32, (HEAD, nk), 1)
                wide = valid if r == 0 else jnp.concatenate([valid, valid], axis=1)
                allowed = (jcol <= irow) & (jcol < wide)
                if r:
                    lower = jnp.concatenate([meta[s, 1:2, :], jnp.ones((1, HEAD), jnp.int32)], axis=1)
                    allowed = allowed & (lower > 0)
                allowed = jnp.concatenate([allowed, allowed], axis=0)
                masked = jnp.where(allowed, scores, -1e30)
                top = jnp.max(masked, axis=1, keepdims=True)
                expo = jnp.where(allowed, jnp.exp((masked - top) * HEAD**-0.5), 0.0).astype(BF16)
                local = jnp.dot(expo, vals, preferred_element_type=F32)
                total = jnp.maximum(local[:, HEAD:], 1.0)
                sq = sigma(q.astype(F32)).astype(BF16)
                retrieved = jnp.dot(sq, mem[s, g], preferred_element_type=F32)
                remembered = retrieved[:, 0:HEAD] / (retrieved[:, HEAD:] + 1.0)
                local = local[:, 0:HEAD] / total
                alive = (lax.broadcasted_iota(jnp.int32, (HEAD, HEAD), 0) + r * HEAD) < valid
                for e in range(2):
                    half = slice(e * HEAD, (e + 1) * HEAD)
                    mixed = gates[e] * remembered[half] + (1.0 - gates[e]) * local[half]
                    stage[j, s, rows, half] = jnp.where(alive, mixed, 0.0).astype(BF16)
        place = pl.ds(pl.multiple_of(c * 4 * CW + j * CW, CW), CW)
        there = pltpu.make_async_remote_copy(
            stage.at[j, 1 - c], out_hbm.at[:, place], osem_s.at[j], osem_r.at[j], device_id=sibling, device_id_type=MESH_ID
        )
        there.start()
        here = pltpu.make_async_copy(stage.at[j, c], out_hbm.at[:, place], osem_l.at[j])
        here.start()
        finals.append((there, here))

    finals = []
    for item in PROGRAM:
        if item == "keys":
            tok_here.wait()
            tok_back.wait_recv()
            project(0, kbuf)
        elif item == "values":
            project(1, vbuf)
        elif item == "delta":
            meta_back.wait_recv()
            delta()
            launch(exchange("x", rx, 0, False))
        elif item == "rows":
            row_totals()
        elif item == "memory":
            memory()
        elif item[0] == "q":
            project(2 + int(item[1]), qbuf.at[int(item[1])])
        elif item[0] == "a":
            attend(int(item[1]))
        else:
            tick(*item)
            if item == (2, 0):
                meta_copy.start()
                tok_copy.start()
                tok_here.start()

    for j, (there, here) in enumerate(finals):
        here.wait()
        there.wait_send()
        arriving = out_hbm.at[:, pl.ds(pl.multiple_of((1 - c) * 4 * CW + j * CW, CW), CW)]
        pltpu.make_async_remote_copy(
            stage.at[j, 1 - c], arriving, osem_s.at[j], osem_r.at[j], device_id=sibling, device_id_type=MESH_ID
        ).wait_recv()
    for one in sent + sends_ + [meta_copy, tok_copy]:
        one.wait_send()


def solution(mesh):
    segs, nz = mesh.shape["seg"], mesh.shape["fsdp"]
    side = {32: 4, 8: 2, 16: 4}[segs]
    dims = {"x": side, "y": segs // 2 // side, "z": nz}

    def shards(tokens, w_query, w_key, value_weight, gate_bias, block_mask, valid_len):
        hbm = pl.BlockSpec(memory_space=pltpu.HBM)
        smem = pl.BlockSpec(memory_space=pltpu.SMEM)
        x, y, nz = dims["x"], dims["y"], dims["z"]
        dma = pltpu.SemaphoreType.DMA
        out = pl.pallas_call(
            functools.partial(body, dims),
            out_shape=jax.ShapeDtypeStruct((SEG, 2048), BF16),
            in_specs=[hbm] * 4 + [smem] * 3,
            out_specs=hbm,
            scratch_shapes=[
                pltpu.VMEM((NCH, y, x, 2, nz, 16, CW), BF16),
                pltpu.VMEM((2, SEG, 4096), BF16),
                pltpu.VMEM((2 * SEG, CW), F32),
                pltpu.VMEM((2, SEG, CW), BF16),
                pltpu.VMEM((2, SEG, CW), BF16),
                pltpu.VMEM((4, 2, SEG, CW), BF16),
                pltpu.VMEM((2, 8, HEAD), jnp.int32),
                pltpu.VMEM((2, HEAD + 16, HEAD), F32),
                pltpu.VMEM((x, 2, HEAD + 16, HEAD), BF16),
                pltpu.VMEM((y, 2, HEAD + 16, HEAD), BF16),
                pltpu.VMEM((2, 2, HEAD, 2 * HEAD), BF16),
                pltpu.VMEM((4, 2, SEG, CW), BF16),
                dma((NCH, 8, 2)),
                dma((NCH, 8, 2)),
                dma((NCH + 1,)),
                dma((NCH + 2,)),
                dma((NCH + 2,)),
                dma((2, 3)),
                dma((2, 3)),
                dma((4,)),
                dma((4,)),
                dma((4,)),
            ],
            compiler_params=pltpu.CompilerParams(
                collective_id=0, has_side_effects=True, vmem_limit_bytes=56 * 1024 * 1024
            ),
        )(tokens[0], w_query, w_key, value_weight, gate_bias, block_mask[0, 0], valid_len)
        return out[None]

    in_specs = (
        P("fsdp", "seg", None),
        P(("seg", "fsdp"), None),
        P(("seg", "fsdp"), None),
        P(("seg", "fsdp"), None),
        P(),
        P("fsdp", "seg", None, None),
        P("fsdp", "seg"),
    )
    return jax.shard_map(
        shards, mesh=mesh, in_specs=in_specs, out_specs=P("fsdp", "seg", None), check_vma=False
    )
```

```python
import functools

import jax
import jax.numpy as jnp
from jax import lax
from jax.experimental import pallas as pl
from jax.experimental.pallas import tpu as pltpu
from jax.sharding import PartitionSpec as P

HEAD = 128
SEG = 256
CW = 256
NCH = 12
ORDERS = ("xyz", "zyx", "zxy", "yxz", "zyx", "zxy")
DIRECT, RING = "direct", "ring"
KINDS = (DIRECT, DIRECT, RING)
MESH_ID = pl.DeviceIdType.MESH
F32 = jnp.float32
BF16 = jnp.bfloat16

PROGRAM = (
    (0, 0), (1, 0), (2, 0), (3, 0), (4, 0), (5, 0), (6, 0), (7, 0), (0, 1), (8, 0), (9, 0), (10, 0), (3, 1),
    (11, 0), (1, 1), (6, 1), (2, 1), (4, 1), (9, 1), (0, 2), (5, 1), (3, 2), (7, 1), (1, 2), (8, 1), (10, 1),
    (2, 2), (11, 1), (4, 2), (0, 3), (5, 2), (3, 3), (0, 4), (1, 3), (7, 2), (3, 4), (2, 3), (8, 2), (0, 5),
    (6, 2), (3, 5), (9, 2), (5, 3), (11, 2), (0, 6), (4, 3), (10, 2), (6, 3), (3, 6), (1, 4), "keys", (2, 4),
    "values", "delta", (9, 3), (6, 4), (5, 4), (7, 3), (8, 3), (9, 4), (4, 4), "q0", (6, 5), "rows", (11, 3),
    (9, 5), (10, 3), (6, 6), "memory", "a0", (7, 4), "q1", "a1", (8, 4), (9, 6), "q2", "a2", (11, 4), (10, 4),
    "q3", "a3",
)


def sigma(v):
    return jnp.where(v > 0, v, jnp.exp(jnp.minimum(v, 0.0)) - 1.0) + 1.0


def body(
    dims,
    tok_hbm, wq_hbm, wk_hbm, wv_hbm, gate_ref, mask_ref, valid_ref,
    out_hbm,
    wst, w, tok, acc, kbuf, vbuf, qbuf, meta, own, rx, ry, mem, stage,
    recv, send, csem_l, csem_s, csem_r, dsem_s, dsem_r, osem_l, osem_s, osem_r,
):
    seg = lax.axis_index("seg")
    z = lax.axis_index("fsdp")
    c = lax.rem(seg, 2)
    x = lax.rem(seg // 2, dims["x"])
    y = seg // (2 * dims["x"])
    pos = {"x": x, "y": y, "z": z}

    def device(xx, yy, cc, zz):
        return {"seg": (yy * dims["x"] + xx) * 2 + cc, "fsdp": zz}

    def shifted(dim, delta):
        at = dict(pos)
        at[dim] = lax.rem(pos[dim] + delta + dims[dim], dims[dim])
        return device(at["x"], at["y"], c, at["z"])

    sibling = device(x, y, 1 - c, z)

    barrier = pltpu.get_barrier_semaphore()
    peers = [sibling]
    for dim in "xyz":
        peers += [shifted(dim, k) for k in range(1, dims[dim])]
    for peer in peers:
        pl.semaphore_signal(barrier, inc=1, device_id=peer, device_id_type=MESH_ID)
    pl.semaphore_wait(barrier, len(peers))

    def columns(core):
        wide = pl.ds(pl.multiple_of(core * CW, CW), CW)
        return (wk_hbm.at[:, wide], wv_hbm.at[:, wide], wq_hbm.at[:, pl.ds(pl.multiple_of(core * 4 * CW, CW), 4 * CW)])

    spans = (slice(0, CW), slice(CW, 2 * CW), slice(2 * CW, 6 * CW))
    locals_, sends_, recvs_ = [], [], []
    for i, span in enumerate(spans):
        there = pltpu.make_async_remote_copy(
            columns(1 - c)[i], wst.at[c, :, span], csem_s.at[i], csem_r.at[i],
            device_id=sibling, device_id_type=MESH_ID,
        )
        there.start()
        here = pltpu.make_async_copy(columns(c)[i], wst.at[c, :, span], csem_l.at[i])
        here.start()
        other = wst.at[1 - c, :, span]
        back = pltpu.make_async_remote_copy(
            other, other, csem_s.at[i], csem_r.at[i], device_id=sibling, device_id_type=MESH_ID
        )
        locals_.append(here)
        sends_.append(there)
        recvs_.append(back)

    row8 = lax.broadcasted_iota(jnp.int32, (8, HEAD), 0)
    meta[c] = jnp.where(row8 == 0, valid_ref[0, 0], mask_ref[1, 0])
    meta_copy = pltpu.make_async_remote_copy(
        meta.at[c], meta.at[c], csem_s.at[3], csem_r.at[3], device_id=sibling, device_id_type=MESH_ID
    )
    meta_back = pltpu.make_async_remote_copy(
        meta.at[1 - c], meta.at[1 - c], csem_s.at[3], csem_r.at[3], device_id=sibling, device_id_type=MESH_ID
    )
    tok_copy = pltpu.make_async_remote_copy(
        tok_hbm, tok.at[c], csem_s.at[4], csem_r.at[4], device_id=sibling, device_id_type=MESH_ID
    )
    tok_back = pltpu.make_async_remote_copy(
        tok.at[1 - c], tok.at[1 - c], csem_s.at[4], csem_r.at[4], device_id=sibling, device_id_type=MESH_ID
    )
    tok_here = pltpu.make_async_copy(tok_hbm, tok.at[c], csem_l.at[3])

    def block(ch, stage_no, index):
        order = ORDERS[ch % 6]
        at = {d: pl.ds(pos[d], 1) for d in "xyz"}
        for d in order[:stage_no]:
            at[d] = slice(None)
        at[order[stage_no]] = pl.ds(index, 1)
        return w.at[ch, at["y"], at["x"], :, at["z"]]

    steps = {}
    for ch in range(NCH):
        steps[ch] = []
        for s, kind in enumerate(KINDS):
            n = dims[ORDERS[ch % 6][s]]
            if kind == DIRECT:
                steps[ch].append([(s, k, 0, -k) for k in range(1, n)])
                continue
            for k in range(1, n // 2 + 1):
                sides = (1, -1) if 2 * k < n else ((1,) if ch // 3 % 2 == 0 else (-1,))
                steps[ch].append([(s, side, -side * (k - 1), -side * k) for side in sides])

    def copies(ch, number, arriving):
        first = sum(len(step) for step in steps[ch][:number])
        made = []
        for m, (s, hop, sent_off, arrive_off) in enumerate(steps[ch][number]):
            dim = ORDERS[ch % 6][s]
            n = dims[dim]
            index = lax.rem(pos[dim] + (arrive_off if arriving else sent_off) + n, n)
            piece = block(ch, s, index)
            made.append(
                pltpu.make_async_remote_copy(
                    piece, piece, send.at[ch, first + m], recv.at[ch, first + m],
                    device_id=shifted(dim, hop), device_id_type=MESH_ID,
                )
            )
        return made

    sent = []

    def tick(ch, number):
        arrived = copies(ch, number - 1, True) if number else []
        leaving = copies(ch, number, False) if number < len(steps[ch]) else []
        paired = number and number < len(steps[ch]) and steps[ch][number][0][0] == steps[ch][number - 1][0][0]
        if paired and len(arrived) == len(leaving):
            for one, two in zip(arrived, leaving):
                one.wait_recv()
                two.start()
        else:
            for one in arrived:
                one.wait_recv()
            for two in leaving:
                two.start()
        sent.extend(leaving)

    def project(ch, dst):
        def part(i, first):
            b = jnp.concatenate([w[ch, i].reshape(1024, HEAD), w[ch + 1, i].reshape(1024, HEAD)], axis=1)
            a = tok[:, :, pl.ds(pl.multiple_of(i * 1024, 1024), 1024)].reshape(2 * SEG, 1024)
            r = jnp.dot(a, b, preferred_element_type=F32)
            if first:
                acc[...] = r
            else:
                acc[...] += r

        part(0, True)

        @pl.loop(1, dims["y"])
        def _(i):
            part(i, False)

        dst[...] = acc[...].astype(BF16).reshape(2, SEG, CW)

    def delta():
        jrow = lax.broadcasted_iota(jnp.int32, (SEG, HEAD), 0)
        for g in range(2):
            cols = slice(g * HEAD, (g + 1) * HEAD)
            both = []
            for s in range(2):
                live = jrow < meta[s, 0:1, :]
                sig = jnp.where(live, sigma(kbuf[s, :, cols].astype(F32)), 0.0)
                zrow = jnp.sum(sig, axis=0, keepdims=True)
                m = lax.dot_general(
                    sig.astype(BF16), vbuf[s, :, cols], (((0,), (0,)), ((), ())), preferred_element_type=F32
                )
                both.append((m, zrow))
            own[g, 0:HEAD, :] = both[0][0]
            own[g, HEAD : HEAD + 16, :] = jnp.broadcast_to(both[0][1], (16, HEAD))
            rx[x, g, 0:HEAD, :] = (both[0][0] + both[1][0]).astype(BF16)
            rx[x, g, HEAD : HEAD + 16, :] = jnp.broadcast_to(both[0][1] + both[1][1], (16, HEAD)).astype(BF16)

    def exchange(dim, buf, number, arriving):
        n = dims[dim]
        copies = []
        for k in range(1, n):
            index = lax.rem(pos[dim] - k + n, n) if arriving else pos[dim]
            copies.append(
                pltpu.make_async_remote_copy(
                    buf.at[index], buf.at[index], dsem_s.at[number, k - 1], dsem_r.at[number, k - 1],
                    device_id=shifted(dim, k), device_id_type=MESH_ID,
                )
            )
        return copies

    def launch(copies):
        for one in copies:
            one.start()
        sent.extend(copies)

    def row_totals():
        for one in exchange("x", rx, 0, True):
            one.wait_recv()
        for g in range(2):
            total = jnp.zeros((HEAD + 16, HEAD), F32)
            for k in range(dims["x"]):
                total = total + rx[k, g].astype(F32)
            ry[y, g] = total.astype(BF16)
        launch(exchange("y", ry, 1, False))

    def memory():
        for one in exchange("y", ry, 1, True):
            one.wait_recv()
        for g in range(2):
            total = jnp.zeros((HEAD + 16, HEAD), F32)
            for k in range(dims["x"]):
                total = total + jnp.where(k < x, rx[k, g].astype(F32), 0.0)
            for k in range(dims["y"]):
                total = total + jnp.where(k < y, ry[k, g].astype(F32), 0.0)
            for s in range(2):
                if s:
                    total = total + own[g]
                mem[s, g, :, 0:HEAD] = total[0:HEAD].astype(BF16)
                zcol = jnp.transpose(jnp.broadcast_to(total[HEAD : HEAD + 1], (HEAD, HEAD)))
                mem[s, g, :, HEAD:] = zcol.astype(BF16)

    ones = jnp.ones((SEG, HEAD), BF16)

    def attend(j):
        g = j // 2
        kcols = slice(g * HEAD, (g + 1) * HEAD)
        gates = []
        for e in range(2):
            bias = jnp.full((1, HEAD), gate_ref[c * 8 + 2 * j + e], F32)
            gates.append(jax.nn.sigmoid(bias))
        for s in range(2):
            valid = meta[s, 0:1, :]
            for r in range(2):
                nk = (r + 1) * HEAD
                rows = slice(r * HEAD, (r + 1) * HEAD)
                q = jnp.concatenate([qbuf[j, s, rows, 0:HEAD], qbuf[j, s, rows, HEAD:]], axis=0)
                keys = kbuf[s, 0:nk, kcols]
                vals = jnp.concatenate([vbuf[s, 0:nk, kcols], ones[0:nk]], axis=1)
                scores = lax.dot_general(q, keys, (((1,), (1,)), ((), ())), preferred_element_type=F32)
                irow = lax.broadcasted_iota(jnp.int32, (HEAD, nk), 0) + r * HEAD
                jcol = lax.broadcasted_iota(jnp.int32, (HEAD, nk), 1)
                wide = valid if r == 0 else jnp.concatenate([valid, valid], axis=1)
                allowed = (jcol <= irow) & (jcol < wide)
                if r:
                    lower = jnp.concatenate([meta[s, 1:2, :], jnp.ones((1, HEAD), jnp.int32)], axis=1)
                    allowed = allowed & (lower > 0)
                allowed = jnp.concatenate([allowed, allowed], axis=0)
                masked = jnp.where(allowed, scores, -1e30)
                top = jnp.max(masked, axis=1, keepdims=True)
                expo = jnp.where(allowed, jnp.exp((masked - top) * HEAD**-0.5), 0.0).astype(BF16)
                local = jnp.dot(expo, vals, preferred_element_type=F32)
                total = jnp.maximum(local[:, HEAD:], 1.0)
                sq = sigma(q.astype(F32)).astype(BF16)
                retrieved = jnp.dot(sq, mem[s, g], preferred_element_type=F32)
                remembered = retrieved[:, 0:HEAD] / (retrieved[:, HEAD:] + 1.0)
                local = local[:, 0:HEAD] / total
                alive = (lax.broadcasted_iota(jnp.int32, (HEAD, HEAD), 0) + r * HEAD) < valid
                for e in range(2):
                    half = slice(e * HEAD, (e + 1) * HEAD)
                    mixed = gates[e] * remembered[half] + (1.0 - gates[e]) * local[half]
                    stage[j, s, rows, half] = jnp.where(alive, mixed, 0.0).astype(BF16)
        place = pl.ds(pl.multiple_of(c * 4 * CW + j * CW, CW), CW)
        there = pltpu.make_async_remote_copy(
            stage.at[j, 1 - c], out_hbm.at[:, place], osem_s.at[j], osem_r.at[j], device_id=sibling, device_id_type=MESH_ID
        )
        there.start()
        here = pltpu.make_async_copy(stage.at[j, c], out_hbm.at[:, place], osem_l.at[j])
        here.start()
        finals.append((there, here))

    finals = []
    for here, back in zip(locals_, recvs_):
        here.wait()
        back.wait_recv()
    for ch in range(NCH):
        w[ch, y, x, :, z] = wst[:, :, ch * HEAD : (ch + 1) * HEAD]
    for item in PROGRAM:
        if item == "keys":
            tok_here.wait()
            tok_back.wait_recv()
            project(0, kbuf)
        elif item == "values":
            project(2, vbuf)
        elif item == "delta":
            meta_back.wait_recv()
            delta()
            launch(exchange("x", rx, 0, False))
        elif item == "rows":
            row_totals()
        elif item == "memory":
            memory()
        elif item[0] == "q":
            project(4 + 2 * int(item[1]), qbuf.at[int(item[1])])
        elif item[0] == "a":
            attend(int(item[1]))
        else:
            tick(*item)
            if item == (NCH - 1, 0):
                meta_copy.start()
                tok_copy.start()
                tok_here.start()

    for j, (there, here) in enumerate(finals):
        here.wait()
        there.wait_send()
        arriving = out_hbm.at[:, pl.ds(pl.multiple_of((1 - c) * 4 * CW + j * CW, CW), CW)]
        pltpu.make_async_remote_copy(
            stage.at[j, 1 - c], arriving, osem_s.at[j], osem_r.at[j], device_id=sibling, device_id_type=MESH_ID
        ).wait_recv()
    for one in sent + sends_ + [meta_copy, tok_copy]:
        one.wait_send()


def solution(mesh):
    segs, nz = mesh.shape["seg"], mesh.shape["fsdp"]
    side = {32: 4, 8: 2, 16: 4}[segs]
    dims = {"x": side, "y": segs // 2 // side, "z": nz}

    def shards(tokens, w_query, w_key, value_weight, gate_bias, block_mask, valid_len):
        hbm = pl.BlockSpec(memory_space=pltpu.HBM)
        smem = pl.BlockSpec(memory_space=pltpu.SMEM)
        x, y, nz = dims["x"], dims["y"], dims["z"]
        dma = pltpu.SemaphoreType.DMA
        out = pl.pallas_call(
            functools.partial(body, dims),
            out_shape=jax.ShapeDtypeStruct((SEG, 2048), BF16),
            in_specs=[hbm] * 4 + [smem] * 3,
            out_specs=hbm,
            scratch_shapes=[
                pltpu.VMEM((2, 16, NCH * HEAD), BF16),
                pltpu.VMEM((NCH, y, x, 2, nz, 16, HEAD), BF16),
                pltpu.VMEM((2, SEG, 4096), BF16),
                pltpu.VMEM((2 * SEG, CW), F32),
                pltpu.VMEM((2, SEG, CW), BF16),
                pltpu.VMEM((2, SEG, CW), BF16),
                pltpu.VMEM((4, 2, SEG, CW), BF16),
                pltpu.VMEM((2, 8, HEAD), jnp.int32),
                pltpu.VMEM((2, HEAD + 16, HEAD), F32),
                pltpu.VMEM((x, 2, HEAD + 16, HEAD), BF16),
                pltpu.VMEM((y, 2, HEAD + 16, HEAD), BF16),
                pltpu.VMEM((2, 2, HEAD, 2 * HEAD), BF16),
                pltpu.VMEM((4, 2, SEG, CW), BF16),
                dma((NCH, x + y + nz - 3)),
                dma((NCH, x + y + nz - 3)),
                dma((4,)),
                dma((5,)),
                dma((5,)),
                dma((2, 3)),
                dma((2, 3)),
                dma((4,)),
                dma((4,)),
                dma((4,)),
            ],
            compiler_params=pltpu.CompilerParams(
                collective_id=0, has_side_effects=True, vmem_limit_bytes=56 * 1024 * 1024
            ),
        )(tokens[0], w_query, w_key, value_weight, gate_bias, block_mask[0, 0], valid_len)
        return out[None]

    in_specs = (
        P("fsdp", "seg", None),
        P(("seg", "fsdp"), None),
        P(("seg", "fsdp"), None),
        P(("seg", "fsdp"), None),
        P(),
        P("fsdp", "seg", None, None),
        P("fsdp", "seg"),
    )
    return jax.shard_map(
        shards, mesh=mesh, in_specs=in_specs, out_specs=P("fsdp", "seg", None), check_vma=False
    )
```

```python
import functools

import jax
import jax.numpy as jnp
from jax import lax
from jax.experimental import pallas as pl
from jax.experimental.pallas import tpu as pltpu
from jax.sharding import PartitionSpec as P

HEAD = 128
SEG = 256
CW = 256
NCH = 12
DIRECT, TWO, RING = "direct", "two", "ring"
ORDERS = ("zyx", "zxy", "zyx", "yxz", "zxy", "xyz", "xzy", "zyx", "xyz", "zxy", "yzx", "yxz")
KINDS = (
    (DIRECT, DIRECT, 2, 0), (DIRECT, DIRECT, 2, 0), (DIRECT, RING, 2, 0),
    (DIRECT, DIRECT, 2, 1), (DIRECT, RING, 2, 0), (DIRECT, RING, 2, 0),
    (DIRECT, RING, 2, 1), (TWO, RING, 2, 1), (DIRECT, DIRECT, 2, 0),
    (TWO, RING, 2, 1), (DIRECT, RING, 2, 1), (DIRECT, DIRECT, 2, 1),
)
MESH_ID = pl.DeviceIdType.MESH
F32 = jnp.float32
LOG2E = 1.4426950408889634
BF16 = jnp.bfloat16

PROGRAM = (
    (5, None, 0), (0, None, 0), (1, None, 0), (2, None, 0), (3, None, 0), (10, None, 0), (6, None, 0), (4, None, 0),
    (7, None, 0), (9, None, 0), (5, None, 1), (3, None, 1), (6, None, 1), (0, None, 1), (10, None, 1), (8, None, 0),
    (1, None, 1), (5, None, 2), (2, None, 1), (3, None, 2), (3, 0, 0), (3, 1, 0), (8, None, 1), (4, None, 1),
    (7, None, 1), (9, None, 1), (0, None, 2), (0, 0, 0), (0, 1, 0), (6, None, 2), (5, None, 3), (5, 0, 0),
    (5, 1, 0), (10, None, 2), (1, None, 2), (1, 0, 0), (1, 1, 0), (2, None, 2), (3, 0, 1), (4, None, 2),
    (8, None, 2), (3, 1, 1), (7, None, 2), (9, None, 2), (6, None, 3), (0, 0, 1), (1, 0, 1), (5, 0, 1),
    (11, None, 0), (5, 1, 1), (0, 1, 1), (10, None, 3), (1, 1, 1), (4, None, 3), (4, 0, 0), (4, 1, 0), (3, 0, 2),
    (2, None, 3), (2, 0, 0), (2, 1, 0), (9, None, 3), (3, 1, 2), (7, None, 3), (6, None, 4), (0, 1, 2), (5, 0, 2),
    (0, 0, 2), (1, 1, 2), (1, 0, 2), ("keys", 0), (5, 1, 2), ("keys", 1), (11, None, 1), ("keys", 2), (10, None, 4),
    ("keys", 3), (2, 0, 1), (3, 0, 3), (8, 0, 0), (4, 0, 1), (3, 1, 3), (8, 1, 0), (6, None, 5), (6, 0, 0),
    (2, 1, 1), (9, None, 4), (5, 0, 3), (4, 1, 1), (6, 1, 0), (7, None, 4), (7, 0, 0), (7, 1, 0), (11, None, 2),
    (11, 0, 0), (3, 0, 4), (5, 1, 3), (11, 1, 0), (10, None, 5), (2, 0, 2), (4, 0, 2), (8, 0, 1), (2, 1, 2),
    (3, 1, 4), ("values", 0), ("values", 1), ("values", 2), (5, 0, 4), ("values", 3), (6, 0, 1), (9, 0, 0),
    ("delta",), (8, 1, 1), (4, 1, 2), (7, 0, 1), (10, 0, 0), (11, 0, 1), (5, 1, 4), ("q", 0, 0), ("q", 0, 1),
    (6, 1, 1), (9, 1, 0), (7, 1, 1), (10, 1, 0), ("q", 0, 2), ("q", 0, 3), (11, 1, 1), ("local", 0, 0),
    ("local", 0, 1), (6, 0, 2), (8, 0, 2), ("rows",), (8, 1, 2), (9, 0, 1), (11, 0, 2), (6, 1, 2), (7, 0, 2),
    (11, 1, 2), (8, 0, 3), (9, 1, 1), (10, 0, 1), (7, 1, 2), ("q", 1, 0), ("q", 1, 1), (8, 1, 3), ("q", 1, 2),
    ("q", 1, 3), ("local", 1, 0), ("local", 1, 1), (11, 0, 3), (10, 1, 1), ("memory",), (8, 0, 4), (11, 1, 3),
    ("finish", 0, 0), ("finish", 0, 1), ("finish", 1, 0), ("finish", 1, 1), (9, 0, 2), (8, 1, 4), (10, 0, 2),
    (9, 1, 2), ("q", 2, 0), ("q", 2, 1), ("q", 2, 2), (11, 0, 4), ("q", 2, 3), ("local", 2, 0), (11, 1, 4),
    ("finish", 2, 0), ("local", 2, 1), ("finish", 2, 1), (10, 1, 2), ("q", 3, 0), ("q", 3, 1), ("q", 3, 2),
    ("q", 3, 3), ("local", 3, 0), ("finish", 3, 0), ("local", 3, 1), ("finish", 3, 1),
)


def sigma(v):
    return jnp.where(v > 0, v, jnp.exp(jnp.minimum(v, 0.0)) - 1.0) + 1.0


def body(
    dims,
    tok_hbm, wq_hbm, wk_hbm, wv_hbm, gate_ref, mask_ref, valid_ref,
    out_ref,
    wst, w, tok, acc, kbuf, vbuf, qbuf, meta, own, rx, ry, mem, loc, stage,
    recv, send, csem_l, csem_s, csem_r, dsem_s, dsem_r, osem_s, osem_r,
):
    seg = lax.axis_index("seg")
    z = lax.axis_index("fsdp")
    c = lax.rem(seg, 2)
    x = lax.rem(seg // 2, dims["x"])
    y = seg // (2 * dims["x"])
    pos = {"x": x, "y": y, "z": z}

    def device(xx, yy, cc, zz):
        return {"seg": (yy * dims["x"] + xx) * 2 + cc, "fsdp": zz}

    def shifted(dim, delta):
        at = dict(pos)
        at[dim] = lax.rem(pos[dim] + delta + dims[dim], dims[dim])
        return device(at["x"], at["y"], c, at["z"])

    sibling = device(x, y, 1 - c, z)

    barrier = pltpu.get_barrier_semaphore()
    peers = [sibling]
    for dim in "xyz":
        peers += [shifted(dim, k) for k in range(1, dims[dim])]
    for peer in peers:
        pl.semaphore_signal(barrier, inc=1, device_id=peer, device_id_type=MESH_ID)
    pl.semaphore_wait(barrier, len(peers))

    def columns(core):
        wide = pl.ds(pl.multiple_of(core * CW, CW), CW)
        return (wk_hbm.at[:, wide], wv_hbm.at[:, wide], wq_hbm.at[:, pl.ds(pl.multiple_of(core * 4 * CW, CW), 4 * CW)])

    spans = (slice(0, CW), slice(CW, 2 * CW), slice(2 * CW, 6 * CW))
    locals_, sends_, recvs_ = [], [], []
    for i, span in enumerate(spans):
        there = pltpu.make_async_remote_copy(
            columns(1 - c)[i], wst.at[c, :, span], csem_s.at[i], csem_r.at[i],
            device_id=sibling, device_id_type=MESH_ID,
        )
        there.start()
        here = pltpu.make_async_copy(columns(c)[i], wst.at[c, :, span], csem_l.at[i])
        here.start()
        other = wst.at[1 - c, :, span]
        back = pltpu.make_async_remote_copy(
            other, other, csem_s.at[i], csem_r.at[i], device_id=sibling, device_id_type=MESH_ID
        )
        locals_.append(here)
        sends_.append(there)
        recvs_.append(back)

    row8 = lax.broadcasted_iota(jnp.int32, (8, HEAD), 0)
    meta[c] = jnp.where(row8 == 0, valid_ref[0, 0], mask_ref[1, 0])
    meta_copy = pltpu.make_async_remote_copy(
        meta.at[c], meta.at[c], csem_s.at[3], csem_r.at[3], device_id=sibling, device_id_type=MESH_ID
    )
    meta_back = pltpu.make_async_remote_copy(
        meta.at[1 - c], meta.at[1 - c], csem_s.at[3], csem_r.at[3], device_id=sibling, device_id_type=MESH_ID
    )
    tok_copy = pltpu.make_async_remote_copy(
        tok_hbm, tok.at[c], csem_s.at[4], csem_r.at[4], device_id=sibling, device_id_type=MESH_ID
    )
    tok_back = pltpu.make_async_remote_copy(
        tok.at[1 - c], tok.at[1 - c], csem_s.at[4], csem_r.at[4], device_id=sibling, device_id_type=MESH_ID
    )
    tok_here = pltpu.make_async_copy(tok_hbm, tok.at[c], csem_l.at[3])

    def block(ch, stage_no, index, sub):
        order = ORDERS[ch]
        at = {d: pl.ds(pos[d], 1) for d in "xyz"}
        for d in order[:stage_no]:
            at[d] = slice(None)
        at[order[stage_no]] = pl.ds(index, 1)
        cores = slice(None) if sub is None else pl.ds(sub, 1)
        return w.at[ch, at["y"], at["x"], cores, at["z"]]

    def stage_steps(ch, s, kind, even):
        n = dims[ORDERS[ch][s]]
        if kind == DIRECT:
            return [[(s, k, 0, -k) for k in range(1, n)]]
        if kind == TWO and n == 8:
            far = (s, 2, -2, -4) if even else (s, -2, 2, 4)
            return [
                [(s, 1, 0, -1), (s, -1, 0, 1), (s, 2, 0, -2), (s, -2, 0, 2)],
                [(s, -1, 2, 3), (s, 1, -2, -3), far],
            ]
        made = []
        for k in range(1, n // 2 + 1):
            sides = (1, -1) if 2 * k < n else ((1,) if even else (-1,))
            made.append([(s, side, -side * (k - 1), -side * k) for side in sides])
        return made

    threads = {}
    for ch in range(NCH):
        k1, k2, subs, odd = KINDS[ch]
        even = not odd
        steps = stage_steps(ch, 0, k1, even) + stage_steps(ch, 1, k2, even)
        threads[ch, None] = (steps, None, 0)
        used = sum(len(step) for step in steps)
        for h in range(subs):
            steps = stage_steps(ch, 2, RING, h == 0 if subs == 2 else even)
            threads[ch, h] = (steps, h if subs == 2 else None, used)
            used += sum(len(step) for step in steps)

    def copies(thread, number, arriving):
        ch = thread[0]
        steps, sub, first = threads[thread]
        first += sum(len(step) for step in steps[:number])
        made = []
        for m, (s, hop, sent_off, arrive_off) in enumerate(steps[number]):
            dim = ORDERS[ch][s]
            n = dims[dim]
            index = lax.rem(pos[dim] + (arrive_off if arriving else sent_off) + n, n)
            piece = block(ch, s, index, sub)
            made.append(
                pltpu.make_async_remote_copy(
                    piece, piece, send.at[ch, first + m], recv.at[ch, first + m],
                    device_id=shifted(dim, hop), device_id_type=MESH_ID,
                )
            )
        return made

    sent = []

    def tick(ch, sub, number):
        thread = (ch, sub)
        steps = threads[thread][0]
        arrived = copies(thread, number - 1, True) if number else []
        leaving = copies(thread, number, False) if number < len(steps) else []
        paired = arrived and leaving and steps[number][0][0] == steps[number - 1][0][0]
        if paired and TWO not in KINDS[ch] and len(arrived) == len(leaving):
            for one, two in zip(arrived, leaving):
                one.wait_recv()
                two.start()
        else:
            for one in arrived:
                one.wait_recv()
            for two in leaving:
                two.start()
        sent.extend(leaving)

    def project(pair, i, dst):
        ch = 2 * pair
        b = jnp.concatenate([w[ch, i].reshape(1024, HEAD), w[ch + 1, i].reshape(1024, HEAD)], axis=1)
        a = tok[:, :, i * 1024 : (i + 1) * 1024].reshape(2 * SEG, 1024)
        r = jnp.dot(a, b, preferred_element_type=F32)
        if i:
            r += acc[pair]
        if i < 3:
            acc[pair] = r
        else:
            dst[...] = r.astype(BF16).reshape(2, SEG, CW)

    def delta():
        jrow = lax.broadcasted_iota(jnp.int32, (SEG, HEAD), 0)
        for g in range(2):
            cols = slice(g * HEAD, (g + 1) * HEAD)
            both = []
            for s in range(2):
                live = jrow < meta[s, 0:1, :]
                sig = jnp.where(live, sigma(kbuf[s, :, cols].astype(F32)), 0.0)
                zrow = jnp.sum(sig, axis=0, keepdims=True)
                m = lax.dot_general(
                    sig.astype(BF16), vbuf[s, :, cols], (((0,), (0,)), ((), ())), preferred_element_type=F32
                )
                both.append((m, zrow))
            own[g, 0:HEAD, :] = both[0][0]
            own[g, HEAD : HEAD + 16, :] = jnp.broadcast_to(both[0][1], (16, HEAD))
            rx[x, g, 0:HEAD, :] = (both[0][0] + both[1][0]).astype(BF16)
            rx[x, g, HEAD : HEAD + 16, :] = jnp.broadcast_to(both[0][1] + both[1][1], (16, HEAD)).astype(BF16)

    def exchange(dim, buf, number, arriving):
        n = dims[dim]
        copies = []
        for k in range(1, n):
            index = lax.rem(pos[dim] - k + n, n) if arriving else pos[dim]
            copies.append(
                pltpu.make_async_remote_copy(
                    buf.at[index], buf.at[index], dsem_s.at[number, k - 1], dsem_r.at[number, k - 1],
                    device_id=shifted(dim, k), device_id_type=MESH_ID,
                )
            )
        return copies

    def launch(copies):
        for one in copies:
            one.start()
        sent.extend(copies)

    def row_totals():
        for one in exchange("x", rx, 0, True):
            one.wait_recv()
        for g in range(2):
            total = jnp.zeros((HEAD + 16, HEAD), F32)
            for k in range(dims["x"]):
                total = total + rx[k, g].astype(F32)
            ry[y, g] = total.astype(BF16)
        launch(exchange("y", ry, 1, False))

    def memory():
        for one in exchange("y", ry, 1, True):
            one.wait_recv()
        for g in range(2):
            total = jnp.zeros((HEAD + 16, HEAD), F32)
            for k in range(dims["x"]):
                total = total + jnp.where(k < x, rx[k, g].astype(F32), 0.0)
            for k in range(dims["y"]):
                total = total + jnp.where(k < y, ry[k, g].astype(F32), 0.0)
            for s in range(2):
                if s:
                    total = total + own[g]
                mem[s, g, :, 0:HEAD] = total[0:HEAD].astype(BF16)
                zcol = jnp.transpose(jnp.broadcast_to(total[HEAD : HEAD + 1], (HEAD, HEAD)))
                mem[s, g, :, HEAD:] = zcol.astype(BF16)

    ones = jnp.ones((SEG, HEAD), BF16)

    def sides(j):
        return [jax.nn.sigmoid(jnp.full((1, HEAD), gate_ref[c * 8 + 2 * j + e], F32)) for e in range(2)]

    def stacked(j, s, rows):
        return jnp.concatenate([qbuf[j, s, rows, 0:HEAD], qbuf[j, s, rows, HEAD:]], axis=0)

    def attend(j, second):
        s = c if second else 1 - c
        kcols = slice(j // 2 * HEAD, (j // 2 + 1) * HEAD)
        gates = sides(j)
        valid = meta[s, 0:1, :]
        for r in range(2):
            nk = (r + 1) * HEAD
            rows = slice(r * HEAD, (r + 1) * HEAD)
            keys = kbuf[s, 0:nk, kcols]
            vals = jnp.concatenate([vbuf[s, 0:nk, kcols], ones[0:nk]], axis=1)
            scores = lax.dot_general(
                stacked(j, s, rows), keys, (((1,), (1,)), ((), ())), preferred_element_type=F32
            )
            irow = lax.broadcasted_iota(jnp.int32, (HEAD, nk), 0) + r * HEAD
            jcol = lax.broadcasted_iota(jnp.int32, (HEAD, nk), 1)
            wide = valid if r == 0 else jnp.concatenate([valid, valid], axis=1)
            allowed = (jcol <= irow) & (jcol < wide)
            if r:
                lower = jnp.concatenate([meta[s, 1:2, :], jnp.ones((1, HEAD), jnp.int32)], axis=1)
                allowed = allowed & (lower > 0)
            allowed = jnp.concatenate([allowed, allowed], axis=0)
            masked = jnp.where(allowed, scores, -1e30)
            top = jnp.max(masked, axis=1, keepdims=True)
            expo = jnp.exp2((masked - top) * (HEAD**-0.5 * LOG2E)).astype(BF16)
            local = jnp.dot(expo, vals, preferred_element_type=F32)
            local = local[:, 0:HEAD] / jnp.maximum(local[:, HEAD:], 1.0)
            for e in range(2):
                half = slice(e * HEAD, (e + 1) * HEAD)
                loc[j, s, rows, half] = (1.0 - gates[e]) * local[half]

    def finish(j, second):
        s = c if second else 1 - c
        gates = sides(j)
        valid = meta[s, 0:1, :]
        first = pl.multiple_of(c * 4 * CW + j * CW, CW)
        for r in range(2):
            rows = slice(r * HEAD, (r + 1) * HEAD)
            sq = sigma(stacked(j, s, rows).astype(F32)).astype(BF16)
            retrieved = jnp.dot(sq, mem[s, j // 2], preferred_element_type=F32)
            remembered = retrieved[:, 0:HEAD] / (retrieved[:, HEAD:] + 1.0)
            alive = (lax.broadcasted_iota(jnp.int32, (HEAD, HEAD), 0) + r * HEAD) < valid
            for e in range(2):
                half = slice(e * HEAD, (e + 1) * HEAD)
                mixed = gates[e] * remembered[half] + loc[j, s, rows, half]
                mixed = jnp.where(alive, mixed, 0.0).astype(BF16)
                if second:
                    out_ref[rows, pl.ds(first + e * HEAD, HEAD)] = mixed
                else:
                    stage[j, rows, half] = mixed
        if not second:
            one = pltpu.make_async_remote_copy(
                stage.at[j], out_ref.at[:, pl.ds(first, CW)], osem_s.at[j], osem_r.at[j],
                device_id=sibling, device_id_type=MESH_ID,
            )
            one.start()
            sent.append(one)

    for here, back in zip(locals_, recvs_):
        here.wait()
        back.wait_recv()
    for ch in range(NCH):
        w[ch, y, x, :, z] = wst[:, :, ch * HEAD : (ch + 1) * HEAD]
    meta_copy.start()
    tok_copy.start()
    tok_here.start()
    for name, *where in PROGRAM:
        if name == "keys":
            if where[0] == 0:
                tok_here.wait()
                tok_back.wait_recv()
            project(0, where[0], kbuf)
        elif name == "values":
            project(1, where[0], vbuf)
        elif name == "q":
            project(2 + where[0], where[1], qbuf.at[where[0]])
        elif name == "delta":
            meta_back.wait_recv()
            delta()
            launch(exchange("x", rx, 0, False))
        elif name == "rows":
            row_totals()
        elif name == "memory":
            memory()
        elif name == "local":
            attend(where[0], where[1])
        elif name == "finish":
            finish(where[0], where[1])
        else:
            tick(name, *where)

    for j in range(4):
        arriving = out_ref.at[:, pl.ds(pl.multiple_of((1 - c) * 4 * CW + j * CW, CW), CW)]
        pltpu.make_async_remote_copy(
            stage.at[j], arriving, osem_s.at[j], osem_r.at[j], device_id=sibling, device_id_type=MESH_ID
        ).wait_recv()
    for one in sent + sends_ + [meta_copy, tok_copy]:
        one.wait_send()


def solution(mesh):
    segs, nz = mesh.shape["seg"], mesh.shape["fsdp"]
    side = {32: 4, 8: 2, 16: 4}[segs]
    dims = {"x": side, "y": segs // 2 // side, "z": nz}

    def shards(tokens, w_query, w_key, value_weight, gate_bias, block_mask, valid_len):
        hbm = pl.BlockSpec(memory_space=pltpu.HBM)
        smem = pl.BlockSpec(memory_space=pltpu.SMEM)
        x, y, nz = dims["x"], dims["y"], dims["z"]
        dma = pltpu.SemaphoreType.DMA
        out = pl.pallas_call(
            functools.partial(body, dims),
            out_shape=pltpu.VMEM((SEG, 2048), BF16),
            in_specs=[hbm] * 4 + [smem] * 3,
            out_specs=pl.BlockSpec(memory_space=pltpu.VMEM),
            scratch_shapes=[
                pltpu.VMEM((2, 16, NCH * HEAD), BF16),
                pltpu.VMEM((NCH, y, x, 2, nz, 16, HEAD), BF16),
                pltpu.VMEM((2, SEG, 4096), BF16),
                pltpu.VMEM((6, 2 * SEG, CW), F32),
                pltpu.VMEM((2, SEG, CW), BF16),
                pltpu.VMEM((2, SEG, CW), BF16),
                pltpu.VMEM((4, 2, SEG, CW), BF16),
                pltpu.VMEM((2, 8, HEAD), jnp.int32),
                pltpu.VMEM((2, HEAD + 16, HEAD), F32),
                pltpu.VMEM((x, 2, HEAD + 16, HEAD), BF16),
                pltpu.VMEM((y, 2, HEAD + 16, HEAD), BF16),
                pltpu.VMEM((2, 2, HEAD, 2 * HEAD), BF16),
                pltpu.VMEM((4, 2, SEG, CW), F32),
                pltpu.VMEM((4, SEG, CW), BF16),
                dma((NCH, 20)),
                dma((NCH, 20)),
                dma((4,)),
                dma((5,)),
                dma((5,)),
                dma((2, 3)),
                dma((2, 3)),
                dma((4,)),
                dma((4,)),
            ],
            compiler_params=pltpu.CompilerParams(
                collective_id=0, has_side_effects=True, vmem_limit_bytes=56 * 1024 * 1024
            ),
        )(tokens[0], w_query, w_key, value_weight, gate_bias, block_mask[0, 0], valid_len)
        return out[None]

    in_specs = (
        P("fsdp", "seg", None),
        P(("seg", "fsdp"), None),
        P(("seg", "fsdp"), None),
        P(("seg", "fsdp"), None),
        P(),
        P("fsdp", "seg", None, None),
        P("fsdp", "seg"),
    )
    return jax.shard_map(
        shards, mesh=mesh, in_specs=in_specs, out_specs=P("fsdp", "seg", None), check_vma=False
    )
```

```python
import functools

import jax
import jax.numpy as jnp
from jax import lax
from jax.experimental import pallas as pl
from jax.experimental.pallas import tpu as pltpu
from jax.sharding import PartitionSpec as P

HEAD = 128
SEG = 256
CW = 256
NCH = 12
DIRECT, TWO, RING = "direct", "two", "ring"
ORDERS = ("zyx", "zxy", "xyz", "xyz", "zyx", "zxy", "yxz", "xyz", "zyx", "zyx", "zxy", "zxy")
KINDS = (
    (DIRECT, DIRECT, 2, 0), (DIRECT, DIRECT, 2, 0), (DIRECT, DIRECT, 1, 1),
    (DIRECT, RING, 1, 0), (TWO, RING, 2, 1), (TWO, RING, 2, 1),
    (DIRECT, RING, 1, 0), (DIRECT, DIRECT, 1, 1), (RING, RING, 2, 0),
    (TWO, RING, 2, 1), (RING, RING, 2, 0), (TWO, RING, 2, 1),
)
MESH_ID = pl.DeviceIdType.MESH
F32 = jnp.float32
LOG2E = 1.4426950408889634
BF16 = jnp.bfloat16

PROGRAM = (
    (3, None, 0), (0, None, 0), (1, None, 0), (2, None, 0), (4, None, 0), (5, None, 0), (6, None, 0), (8, None, 0),
    (10, None, 0), (3, None, 1), (2, None, 1), (9, None, 0), (11, None, 0), (7, None, 0), (0, None, 1),
    (6, None, 1), (1, None, 1), (3, None, 2), (4, None, 1), (5, None, 1), (8, None, 1), (10, None, 1), (7, None, 1),
    (2, None, 2), (2, 0, 0), (9, None, 1), (6, None, 2), (11, None, 1), (4, None, 2), (5, None, 2), (8, None, 2),
    (10, None, 2), (0, None, 2), (0, 0, 0), (0, 1, 0), (3, None, 3), (3, 0, 0), (1, None, 2), (1, 0, 0), (1, 1, 0),
    (6, None, 3), (7, None, 2), (2, 0, 1), (9, None, 2), (5, None, 3), (4, None, 3), (11, None, 2), (8, None, 3),
    (10, None, 3), (0, 0, 1), (1, 0, 1), (3, 0, 1), (0, 1, 1), (8, None, 4), (10, None, 4), (1, 1, 1), (2, 0, 2),
    (5, None, 4), (5, 0, 0), (5, 1, 0), (9, None, 3), (4, None, 4), (4, 0, 0), (4, 1, 0), (11, None, 3), (3, 0, 2),
    (0, 0, 2), (1, 0, 2), (0, 1, 2), (8, None, 5), (2, 0, 3), (6, 0, 0), (1, 1, 2), ("keys", 0), (10, None, 5),
    ("keys", 1), ("keys", 2), ("keys", 3), (3, 0, 3), (7, 0, 0), (5, 0, 1), (4, 0, 1), (2, 0, 4), (10, None, 6),
    (10, 0, 0), (4, 1, 1), (5, 1, 1), (10, 1, 0), (8, None, 6), (8, 0, 0), (8, 1, 0), (9, None, 4), (9, 0, 0),
    (11, None, 4), (11, 0, 0), (3, 0, 4), ("values", 0), ("values", 1), (6, 0, 1), ("values", 2), ("values", 3),
    (4, 0, 2), ("delta",), (5, 0, 2), (7, 0, 1), (4, 1, 2), (10, 0, 1), (11, 1, 0), ("q", 3, 0), (6, 0, 2),
    (5, 1, 2), ("q", 0, 0), (8, 0, 1), (9, 1, 0), ("q", 0, 1), ("q", 0, 2), ("q", 0, 3), ("q", 2, 0), ("local", 0),
    (10, 1, 1), (8, 1, 1), (7, 0, 2), (6, 0, 3), (11, 0, 1), (9, 0, 1), (10, 0, 2), (7, 0, 3), (8, 0, 2),
    (11, 1, 1), ("q", 3, 1), ("q", 3, 2), ("rows",), (6, 0, 4), (10, 1, 2), (9, 1, 1), ("q", 2, 1), (11, 0, 2),
    ("q", 2, 2), (7, 0, 4), ("q", 1, 0), ("q", 1, 1), ("q", 1, 2), ("q", 1, 3), (8, 1, 2), (11, 1, 2), ("q", 3, 3),
    (9, 0, 2), ("local", 1), ("local", 3), (9, 1, 2), ("q", 2, 3), ("local", 2), ("memory",), ("finish", 0),
    ("finish", 1), ("finish", 2), ("finish", 3),
)


def sigma(v):
    return jnp.where(v > 0, v, jnp.exp(jnp.minimum(v, 0.0)) - 1.0) + 1.0


def body(
    dims,
    tok_hbm, wq_hbm, wk_hbm, wv_hbm, gate_ref, mask_ref, valid_ref,
    out_ref,
    wst, w, tok, acc, kbuf, vbuf, qbuf, meta, own, rx, ry, mem, loc, stage,
    recv, send, csem_l, csem_s, csem_r, dsem_s, dsem_r, osem_s, osem_r,
):
    seg = lax.axis_index("seg")
    z = lax.axis_index("fsdp")
    c = lax.rem(seg, 2)
    x = lax.rem(seg // 2, dims["x"])
    y = seg // (2 * dims["x"])
    pos = {"x": x, "y": y, "z": z}

    def device(xx, yy, cc, zz):
        return {"seg": (yy * dims["x"] + xx) * 2 + cc, "fsdp": zz}

    def shifted(dim, delta):
        at = dict(pos)
        at[dim] = lax.rem(pos[dim] + delta + dims[dim], dims[dim])
        return device(at["x"], at["y"], c, at["z"])

    sibling = device(x, y, 1 - c, z)

    barrier = pltpu.get_barrier_semaphore()
    peers = [sibling]
    for dim in "xyz":
        peers += [shifted(dim, k) for k in range(1, dims[dim])]
    for peer in peers:
        pl.semaphore_signal(barrier, inc=1, device_id=peer, device_id_type=MESH_ID)
    pl.semaphore_wait(barrier, len(peers))

    def columns(core):
        wide = pl.ds(pl.multiple_of(core * CW, CW), CW)
        return (wk_hbm.at[:, wide], wv_hbm.at[:, wide], wq_hbm.at[:, pl.ds(pl.multiple_of(core * 4 * CW, CW), 4 * CW)])

    spans = (slice(0, CW), slice(CW, 2 * CW), slice(2 * CW, 6 * CW))
    locals_, sends_, recvs_ = [], [], []
    for i, span in enumerate(spans):
        there = pltpu.make_async_remote_copy(
            columns(1 - c)[i], wst.at[c, :, span], csem_s.at[i], csem_r.at[i],
            device_id=sibling, device_id_type=MESH_ID,
        )
        there.start()
        here = pltpu.make_async_copy(columns(c)[i], wst.at[c, :, span], csem_l.at[i])
        here.start()
        other = wst.at[1 - c, :, span]
        back = pltpu.make_async_remote_copy(
            other, other, csem_s.at[i], csem_r.at[i], device_id=sibling, device_id_type=MESH_ID
        )
        locals_.append(here)
        sends_.append(there)
        recvs_.append(back)

    row8 = lax.broadcasted_iota(jnp.int32, (8, HEAD), 0)
    meta[c] = jnp.where(row8 == 0, valid_ref[0, 0], mask_ref[1, 0])
    meta_copy = pltpu.make_async_remote_copy(
        meta.at[c], meta.at[c], csem_s.at[3], csem_r.at[3], device_id=sibling, device_id_type=MESH_ID
    )
    meta_back = pltpu.make_async_remote_copy(
        meta.at[1 - c], meta.at[1 - c], csem_s.at[3], csem_r.at[3], device_id=sibling, device_id_type=MESH_ID
    )
    tok_copy = pltpu.make_async_remote_copy(
        tok_hbm, tok.at[c], csem_s.at[4], csem_r.at[4], device_id=sibling, device_id_type=MESH_ID
    )
    tok_back = pltpu.make_async_remote_copy(
        tok.at[1 - c], tok.at[1 - c], csem_s.at[4], csem_r.at[4], device_id=sibling, device_id_type=MESH_ID
    )
    tok_here = pltpu.make_async_copy(tok_hbm, tok.at[c], csem_l.at[3])

    def block(ch, stage_no, index, sub):
        order = ORDERS[ch]
        at = {d: pl.ds(pos[d], 1) for d in "xyz"}
        for d in order[:stage_no]:
            at[d] = slice(None)
        at[order[stage_no]] = pl.ds(index, 1)
        cores = slice(None) if sub is None else pl.ds(sub, 1)
        return w.at[ch, at["y"], at["x"], cores, at["z"]]

    def stage_steps(ch, s, kind, even):
        n = dims[ORDERS[ch][s]]
        if kind == DIRECT:
            return [[(s, k, 0, -k) for k in range(1, n)]]
        if kind == TWO and n == 8:
            far = (s, 2, -2, -4) if even else (s, -2, 2, 4)
            return [
                [(s, 1, 0, -1), (s, -1, 0, 1), (s, 2, 0, -2), (s, -2, 0, 2)],
                [(s, -1, 2, 3), (s, 1, -2, -3), far],
            ]
        made = []
        for k in range(1, n // 2 + 1):
            sides = (1, -1) if 2 * k < n else ((1,) if even else (-1,))
            made.append([(s, side, -side * (k - 1), -side * k) for side in sides])
        return made

    threads = {}
    for ch in range(NCH):
        k1, k2, subs, odd = KINDS[ch]
        even = not odd
        steps = stage_steps(ch, 0, k1, even) + stage_steps(ch, 1, k2, even)
        threads[ch, None] = (steps, None, 0)
        used = sum(len(step) for step in steps)
        for h in range(subs):
            steps = stage_steps(ch, 2, RING, h == 0 if subs == 2 else even)
            threads[ch, h] = (steps, h if subs == 2 else None, used)
            used += sum(len(step) for step in steps)

    def copies(thread, number, arriving):
        ch = thread[0]
        steps, sub, first = threads[thread]
        first += sum(len(step) for step in steps[:number])
        made = []
        for m, (s, hop, sent_off, arrive_off) in enumerate(steps[number]):
            dim = ORDERS[ch][s]
            n = dims[dim]
            index = lax.rem(pos[dim] + (arrive_off if arriving else sent_off) + n, n)
            piece = block(ch, s, index, sub)
            made.append(
                pltpu.make_async_remote_copy(
                    piece, piece, send.at[ch, first + m], recv.at[ch, first + m],
                    device_id=shifted(dim, hop), device_id_type=MESH_ID,
                )
            )
        return made

    sent, flying = [], {}

    def tick(ch, sub, number):
        thread = (ch, sub)
        steps = threads[thread][0]
        arrived = copies(thread, number - 1, True) if number else []
        leaving = copies(thread, number, False) if number < len(steps) else []
        paired = arrived and leaving and steps[number][0][0] == steps[number - 1][0][0]
        if paired and TWO not in KINDS[ch] and len(arrived) == len(leaving):
            for one, two in zip(arrived, leaving):
                one.wait_recv()
                two.start()
        else:
            for one in arrived:
                one.wait_recv()
            for two in leaving:
                two.start()
        for one in flying.pop(thread, ()):
            one.wait_send()
        flying[thread] = leaving

    def project(pair, i, dst):
        ch = 2 * pair
        last = {ORDERS[ch][2], ORDERS[ch + 1][2]}
        if last == {"x"}:
            at = lax.rem(x + (0, 1, 3, 2)[i], 4)
            b = [w[ch + e, :, at].reshape(1024, HEAD) for e in range(2)]
            a = [tok[:, :, pl.ds(pl.multiple_of(k * 1024 + at * 256, 256), 256)] for k in range(4)]
            a = jnp.concatenate(a, axis=2)
        else:
            at = lax.rem(y + (0, 1, 3, 2)[i], 4) if last == {"y"} else i
            b = [w[ch + e, at].reshape(1024, HEAD) for e in range(2)]
            a = tok[:, :, pl.ds(pl.multiple_of(at * 1024, 1024), 1024)]
        a = a.reshape(2 * SEG, 1024)
        b = jnp.concatenate(b, axis=1)
        r = jnp.dot(a, b, preferred_element_type=F32)
        if i:
            r += acc[pair]
        if i < 3:
            acc[pair] = r
        else:
            dst[...] = r.astype(BF16).reshape(2, SEG, CW)

    def delta():
        jrow = lax.broadcasted_iota(jnp.int32, (SEG, HEAD), 0)
        for g in range(2):
            cols = slice(g * HEAD, (g + 1) * HEAD)
            both = []
            for s in range(2):
                live = jrow < meta[s, 0:1, :]
                sig = jnp.where(live, sigma(kbuf[s, :, cols].astype(F32)), 0.0)
                zrow = jnp.sum(sig, axis=0, keepdims=True)
                m = lax.dot_general(
                    sig.astype(BF16), vbuf[s, :, cols], (((0,), (0,)), ((), ())), preferred_element_type=F32
                )
                both.append((m, zrow))
            own[g, 0:HEAD, :] = both[0][0]
            own[g, HEAD : HEAD + 16, :] = jnp.broadcast_to(both[0][1], (16, HEAD))
            rx[x, g, 0:HEAD, :] = (both[0][0] + both[1][0]).astype(BF16)
            rx[x, g, HEAD : HEAD + 16, :] = jnp.broadcast_to(both[0][1] + both[1][1], (16, HEAD)).astype(BF16)

    def exchange(dim, buf, number, arriving):
        n = dims[dim]
        copies = []
        for k in range(1, n):
            index = lax.rem(pos[dim] - k + n, n) if arriving else pos[dim]
            copies.append(
                pltpu.make_async_remote_copy(
                    buf.at[index], buf.at[index], dsem_s.at[number, k - 1], dsem_r.at[number, k - 1],
                    device_id=shifted(dim, k), device_id_type=MESH_ID,
                )
            )
        return copies

    def launch(copies):
        for one in copies:
            one.start()
        sent.extend(copies)

    def row_totals():
        for one in exchange("x", rx, 0, True):
            one.wait_recv()
        for g in range(2):
            total = jnp.zeros((HEAD + 16, HEAD), F32)
            for k in range(dims["x"]):
                total = total + rx[k, g].astype(F32)
            ry[y, g] = total.astype(BF16)
        launch(exchange("y", ry, 1, False))

    def memory():
        for one in exchange("y", ry, 1, True):
            one.wait_recv()
        for g in range(2):
            total = jnp.zeros((HEAD + 16, HEAD), F32)
            for k in range(dims["x"]):
                total = total + jnp.where(k < x, rx[k, g].astype(F32), 0.0)
            for k in range(dims["y"]):
                total = total + jnp.where(k < y, ry[k, g].astype(F32), 0.0)
            for s in range(2):
                if s:
                    total = total + own[g]
                mem[s, g, :, 0:HEAD] = total[0:HEAD].astype(BF16)
                zcol = jnp.transpose(jnp.broadcast_to(total[HEAD : HEAD + 1], (HEAD, HEAD)))
                mem[s, g, :, HEAD:] = zcol.astype(BF16)

    ones = jnp.ones((SEG, HEAD), BF16)

    def sides(j):
        return [jax.nn.sigmoid(jnp.full((1, HEAD), gate_ref[c * 8 + 2 * j + e], F32)) for e in range(2)]

    def stacked(j, s, rows):
        return jnp.concatenate([qbuf[j, s, rows, 0:HEAD], qbuf[j, s, rows, HEAD:]], axis=0)

    def attend(j):
        kcols = slice(j // 2 * HEAD, (j // 2 + 1) * HEAD)
        gates = sides(j)
        blocks = [(s, r, (r + 1) * HEAD, slice(r * HEAD, (r + 1) * HEAD)) for r in (1, 0) for s in range(2)]
        scores = [
            lax.dot_general(
                stacked(j, s, rows), kbuf[s, 0:nk, kcols], (((1,), (1,)), ((), ())), preferred_element_type=F32
            )
            for s, r, nk, rows in blocks
        ]
        expo = []
        for (s, r, nk, rows), score in zip(blocks, scores):
            valid = meta[s, 0:1, :]
            irow = lax.broadcasted_iota(jnp.int32, (HEAD, nk), 0) + r * HEAD
            jcol = lax.broadcasted_iota(jnp.int32, (HEAD, nk), 1)
            wide = valid if r == 0 else jnp.concatenate([valid, valid], axis=1)
            allowed = (jcol <= irow) & (jcol < wide)
            if r:
                lower = jnp.concatenate([meta[s, 1:2, :], jnp.ones((1, HEAD), jnp.int32)], axis=1)
                allowed = allowed & (lower > 0)
            allowed = jnp.concatenate([allowed, allowed], axis=0)
            masked = jnp.where(allowed, score, -1e30)
            top = jnp.max(masked, axis=1, keepdims=True)
            expo.append(jnp.exp2((masked - top) * (HEAD**-0.5 * LOG2E)).astype(BF16))
        local = [
            jnp.dot(
                weights, jnp.concatenate([vbuf[s, 0:nk, kcols], ones[0:nk]], axis=1), preferred_element_type=F32
            )
            for (s, r, nk, rows), weights in zip(blocks, expo)
        ]
        for (s, r, nk, rows), one in zip(blocks, local):
            one = one[:, 0:HEAD] / jnp.maximum(one[:, HEAD:], 1.0)
            for e in range(2):
                half = slice(e * HEAD, (e + 1) * HEAD)
                loc[j, s, rows, half] = (1.0 - gates[e]) * one[half]

    def finish(j, second):
        s = c if second else 1 - c
        gates = sides(j)
        valid = meta[s, 0:1, :]
        first = pl.multiple_of(c * 4 * CW + j * CW, CW)
        for r in range(2):
            rows = slice(r * HEAD, (r + 1) * HEAD)
            sq = sigma(stacked(j, s, rows).astype(F32)).astype(BF16)
            retrieved = jnp.dot(sq, mem[s, j // 2], preferred_element_type=F32)
            remembered = retrieved[:, 0:HEAD] / (retrieved[:, HEAD:] + 1.0)
            alive = (lax.broadcasted_iota(jnp.int32, (HEAD, HEAD), 0) + r * HEAD) < valid
            for e in range(2):
                half = slice(e * HEAD, (e + 1) * HEAD)
                mixed = gates[e] * remembered[half] + loc[j, s, rows, half]
                mixed = jnp.where(alive, mixed, 0.0).astype(BF16)
                if second:
                    out_ref[rows, pl.ds(first + e * HEAD, HEAD)] = mixed
                else:
                    stage[j, rows, half] = mixed
        if not second:
            one = pltpu.make_async_remote_copy(
                stage.at[j], out_ref.at[:, pl.ds(first, CW)], osem_s.at[j], osem_r.at[j],
                device_id=sibling, device_id_type=MESH_ID,
            )
            one.start()
            sent.append(one)

    for here, back in zip(locals_, recvs_):
        here.wait()
        back.wait_recv()
    for ch in range(NCH):
        w[ch, y, x, :, z] = wst[:, :, ch * HEAD : (ch + 1) * HEAD]
    meta_copy.start()
    tok_copy.start()
    tok_here.start()
    for name, *where in PROGRAM:
        if name == "keys":
            if where[0] == 0:
                tok_here.wait()
                tok_back.wait_recv()
            project(0, where[0], kbuf)
        elif name == "values":
            project(1, where[0], vbuf)
        elif name == "q":
            project(2 + where[0], where[1], qbuf.at[where[0]])
        elif name == "delta":
            meta_back.wait_recv()
            delta()
            launch(exchange("x", rx, 0, False))
        elif name == "rows":
            row_totals()
        elif name == "memory":
            memory()
        elif name == "local":
            attend(where[0])
        elif name == "finish":
            finish(where[0], False)
            finish(where[0], True)
        else:
            tick(name, *where)

    for j in range(4):
        arriving = out_ref.at[:, pl.ds(pl.multiple_of((1 - c) * 4 * CW + j * CW, CW), CW)]
        pltpu.make_async_remote_copy(
            stage.at[j], arriving, osem_s.at[j], osem_r.at[j], device_id=sibling, device_id_type=MESH_ID
        ).wait_recv()
    for one in sent + sends_ + [meta_copy, tok_copy]:
        one.wait_send()


def solution(mesh):
    segs, nz = mesh.shape["seg"], mesh.shape["fsdp"]
    side = {32: 4, 8: 2, 16: 4}[segs]
    dims = {"x": side, "y": segs // 2 // side, "z": nz}

    def shards(tokens, w_query, w_key, value_weight, gate_bias, block_mask, valid_len):
        hbm = pl.BlockSpec(memory_space=pltpu.HBM)
        smem = pl.BlockSpec(memory_space=pltpu.SMEM)
        x, y, nz = dims["x"], dims["y"], dims["z"]
        dma = pltpu.SemaphoreType.DMA
        out = pl.pallas_call(
            functools.partial(body, dims),
            out_shape=pltpu.VMEM((SEG, 2048), BF16),
            in_specs=[hbm] * 4 + [smem] * 3,
            out_specs=pl.BlockSpec(memory_space=pltpu.VMEM),
            scratch_shapes=[
                pltpu.VMEM((2, 16, NCH * HEAD), BF16),
                pltpu.VMEM((NCH, y, x, 2, nz, 16, HEAD), BF16),
                pltpu.VMEM((2, SEG, 4096), BF16),
                pltpu.VMEM((6, 2 * SEG, CW), F32),
                pltpu.VMEM((2, SEG, CW), BF16),
                pltpu.VMEM((2, SEG, CW), BF16),
                pltpu.VMEM((4, 2, SEG, CW), BF16),
                pltpu.VMEM((2, 8, HEAD), jnp.int32),
                pltpu.VMEM((2, HEAD + 16, HEAD), F32),
                pltpu.VMEM((x, 2, HEAD + 16, HEAD), BF16),
                pltpu.VMEM((y, 2, HEAD + 16, HEAD), BF16),
                pltpu.VMEM((2, 2, HEAD, 2 * HEAD), BF16),
                pltpu.VMEM((4, 2, SEG, CW), F32),
                pltpu.VMEM((4, SEG, CW), BF16),
                dma((NCH, 20)),
                dma((NCH, 20)),
                dma((4,)),
                dma((5,)),
                dma((5,)),
                dma((2, 3)),
                dma((2, 3)),
                dma((4,)),
                dma((4,)),
            ],
            compiler_params=pltpu.CompilerParams(
                collective_id=0, has_side_effects=True, vmem_limit_bytes=56 * 1024 * 1024
            ),
        )(tokens[0], w_query, w_key, value_weight, gate_bias, block_mask[0, 0], valid_len)
        return out[None]

    in_specs = (
        P("fsdp", "seg", None),
        P(("seg", "fsdp"), None),
        P(("seg", "fsdp"), None),
        P(("seg", "fsdp"), None),
        P(),
        P("fsdp", "seg", None, None),
        P("fsdp", "seg"),
    )
    return jax.shard_map(
        shards, mesh=mesh, in_specs=in_specs, out_specs=P("fsdp", "seg", None), check_vma=False
    )
```

```python
import functools

import jax
import jax.numpy as jnp
from jax import lax
from jax.experimental import pallas as pl
from jax.experimental.pallas import tpu as pltpu
from jax.sharding import PartitionSpec as P

HEAD = 128
SEG = 256
CW = 256
NCH = 12
DIRECT, TWO, RING = "direct", "two", "ring"
ORDERS = ("zyx", "zxy", "xyz", "xyz", "zyx", "zxy", "yxz", "xyz", "zyx", "zyx", "zxy", "zxy")
KINDS = (
    (DIRECT, DIRECT, 2, 0), (DIRECT, DIRECT, 2, 0), (DIRECT, DIRECT, 1, 1),
    (DIRECT, RING, 1, 0), (TWO, RING, 2, 1), (TWO, RING, 2, 1),
    (DIRECT, RING, 1, 0), (DIRECT, DIRECT, 1, 1), (RING, RING, 2, 0),
    (TWO, RING, 2, 1), (RING, RING, 2, 0), (TWO, RING, 2, 1),
)
MESH_ID = pl.DeviceIdType.MESH
F32 = jnp.float32
LOG2E = 1.4426950408889634
BF16 = jnp.bfloat16

PROGRAM = (
    (3, None, 0), (0, None, 0), (1, None, 0), (2, None, 0), (4, None, 0), (5, None, 0), (6, None, 0), (8, None, 0),
    (10, None, 0), (3, None, 1), (2, None, 1), (9, None, 0), (11, None, 0), (7, None, 0), (0, None, 1),
    (6, None, 1), (1, None, 1), (3, None, 2), (4, None, 1), (5, None, 1), (8, None, 1), (10, None, 1), (7, None, 1),
    (2, None, 2), (2, 0, 0), (9, None, 1), (6, None, 2), (11, None, 1), (4, None, 2), (5, None, 2), (8, None, 2),
    (10, None, 2), (0, None, 2), (0, 0, 0), (0, 1, 0), (3, None, 3), (3, 0, 0), (1, None, 2), (1, 0, 0), (1, 1, 0),
    (6, None, 3), (7, None, 2), (2, 0, 1), (9, None, 2), (5, None, 3), (4, None, 3), (11, None, 2), (8, None, 3),
    (10, None, 3), (0, 0, 1), (1, 0, 1), (3, 0, 1), (0, 1, 1), (8, None, 4), (10, None, 4), (1, 1, 1), (2, 0, 2),
    (5, None, 4), (5, 0, 0), (5, 1, 0), (9, None, 3), (4, None, 4), (4, 0, 0), (4, 1, 0), (11, None, 3), (3, 0, 2),
    (0, 0, 2), (1, 0, 2), (0, 1, 2), (8, None, 5), (2, 0, 3), (6, 0, 0), (1, 1, 2), ("keys", 0), (10, None, 5),
    ("keys", 1), ("keys", 2), ("keys", 3), (3, 0, 3), (7, 0, 0), (5, 0, 1), (4, 0, 1), (2, 0, 4), (10, None, 6),
    (10, 0, 0), (4, 1, 1), (5, 1, 1), (10, 1, 0), (8, None, 6), (8, 0, 0), (8, 1, 0), (9, None, 4), (9, 0, 0),
    (11, None, 4), (11, 0, 0), (3, 0, 4), ("values", 0), ("values", 1), (6, 0, 1), ("values", 2), ("values", 3),
    (4, 0, 2), ("delta",), (5, 0, 2), (7, 0, 1), (4, 1, 2), (10, 0, 1), (11, 1, 0), ("q", 3, 0), (6, 0, 2),
    (5, 1, 2), ("q", 0, 0), (8, 0, 1), (9, 1, 0), ("q", 0, 1), ("q", 0, 2), ("q", 0, 3), ("q", 2, 0), ("local", 0),
    (10, 1, 1), (8, 1, 1), (7, 0, 2), (6, 0, 3), (11, 0, 1), (9, 0, 1), (10, 0, 2), (7, 0, 3), (8, 0, 2),
    (11, 1, 1), ("q", 3, 1), ("q", 3, 2), ("rows",), (6, 0, 4), (10, 1, 2), (9, 1, 1), ("q", 2, 1), (11, 0, 2),
    ("q", 2, 2), (7, 0, 4), ("q", 1, 0), ("q", 1, 1), ("q", 1, 2), ("q", 1, 3), (8, 1, 2), (11, 1, 2), ("q", 3, 3),
    (9, 0, 2), ("local", 1), ("local", 3), (9, 1, 2), ("q", 2, 3), ("local", 2), ("memory",), ("finish", 0),
    ("finish", 1), ("finish", 2), ("finish", 3),
)


def sigma(v):
    return jnp.where(v > 0, v, jnp.exp(jnp.minimum(v, 0.0)) - 1.0) + 1.0


def body(
    dims,
    tok_hbm, wq_hbm, wk_hbm, wv_hbm, gate_ref, mask_ref, valid_ref,
    out_ref,
    wst, w, tok, acc, kbuf, vbuf, qbuf, meta, own, rx, ry, mem, loc, stage,
    recv, send, csem_l, csem_s, csem_r, dsem_s, dsem_r, osem_s, osem_r,
):
    seg = lax.axis_index("seg")
    z = lax.axis_index("fsdp")
    c = lax.rem(seg, 2)
    x = lax.rem(seg // 2, dims["x"])
    y = seg // (2 * dims["x"])
    pos = {"x": x, "y": y, "z": z}

    def device(xx, yy, cc, zz):
        return {"seg": (yy * dims["x"] + xx) * 2 + cc, "fsdp": zz}

    def shifted(dim, delta):
        at = dict(pos)
        at[dim] = lax.rem(pos[dim] + delta + dims[dim], dims[dim])
        return device(at["x"], at["y"], c, at["z"])

    sibling = device(x, y, 1 - c, z)

    barrier = pltpu.get_barrier_semaphore()
    peers = [sibling]
    for dim in "xyz":
        peers += [shifted(dim, k) for k in range(1, dims[dim])]
    for peer in peers:
        pl.semaphore_signal(barrier, inc=1, device_id=peer, device_id_type=MESH_ID)
    pl.semaphore_wait(barrier, len(peers))

    def columns(core):
        wide = pl.ds(pl.multiple_of(core * CW, CW), CW)
        return (wk_hbm.at[:, wide], wv_hbm.at[:, wide], wq_hbm.at[:, pl.ds(pl.multiple_of(core * 4 * CW, CW), 4 * CW)])

    spans = (slice(0, CW), slice(CW, 2 * CW), slice(2 * CW, 6 * CW))
    locals_, sends_, recvs_ = [], [], []
    for i, span in enumerate(spans):
        there = pltpu.make_async_remote_copy(
            columns(1 - c)[i], wst.at[c, :, span], csem_s.at[i], csem_r.at[i],
            device_id=sibling, device_id_type=MESH_ID,
        )
        there.start()
        here = pltpu.make_async_copy(columns(c)[i], wst.at[c, :, span], csem_l.at[i])
        here.start()
        other = wst.at[1 - c, :, span]
        back = pltpu.make_async_remote_copy(
            other, other, csem_s.at[i], csem_r.at[i], device_id=sibling, device_id_type=MESH_ID
        )
        locals_.append(here)
        sends_.append(there)
        recvs_.append(back)

    row8 = lax.broadcasted_iota(jnp.int32, (8, HEAD), 0)
    meta[c] = jnp.where(row8 == 0, valid_ref[0, 0], mask_ref[1, 0])
    meta_copy = pltpu.make_async_remote_copy(
        meta.at[c], meta.at[c], csem_s.at[3], csem_r.at[3], device_id=sibling, device_id_type=MESH_ID
    )
    meta_back = pltpu.make_async_remote_copy(
        meta.at[1 - c], meta.at[1 - c], csem_s.at[3], csem_r.at[3], device_id=sibling, device_id_type=MESH_ID
    )
    tok_copy = pltpu.make_async_remote_copy(
        tok_hbm, tok.at[c], csem_s.at[4], csem_r.at[4], device_id=sibling, device_id_type=MESH_ID
    )
    tok_back = pltpu.make_async_remote_copy(
        tok.at[1 - c], tok.at[1 - c], csem_s.at[4], csem_r.at[4], device_id=sibling, device_id_type=MESH_ID
    )
    tok_here = pltpu.make_async_copy(tok_hbm, tok.at[c], csem_l.at[3])

    def block(ch, stage_no, index, sub):
        order = ORDERS[ch]
        at = {d: pl.ds(pos[d], 1) for d in "xyz"}
        for d in order[:stage_no]:
            at[d] = slice(None)
        at[order[stage_no]] = pl.ds(index, 1)
        cores = slice(None) if sub is None else pl.ds(sub, 1)
        return w.at[ch, at["y"], at["x"], cores, at["z"]]

    def stage_steps(ch, s, kind, even):
        n = dims[ORDERS[ch][s]]
        if kind == DIRECT:
            return [[(s, k, 0, -k) for k in range(1, n)]]
        if kind == TWO and n == 8:
            far = (s, 2, -2, -4) if even else (s, -2, 2, 4)
            return [
                [(s, 1, 0, -1), (s, -1, 0, 1), (s, 2, 0, -2), (s, -2, 0, 2)],
                [(s, -1, 2, 3), (s, 1, -2, -3), far],
            ]
        made = []
        for k in range(1, n // 2 + 1):
            sides = (1, -1) if 2 * k < n else ((1,) if even else (-1,))
            made.append([(s, side, -side * (k - 1), -side * k) for side in sides])
        return made

    threads = {}
    for ch in range(NCH):
        k1, k2, subs, odd = KINDS[ch]
        even = not odd
        steps = stage_steps(ch, 0, k1, even) + stage_steps(ch, 1, k2, even)
        threads[ch, None] = (steps, None, 0)
        used = sum(len(step) for step in steps)
        for h in range(subs):
            steps = stage_steps(ch, 2, RING, h == 0 if subs == 2 else even)
            threads[ch, h] = (steps, h if subs == 2 else None, used)
            used += sum(len(step) for step in steps)

    def copies(thread, number, arriving):
        ch = thread[0]
        steps, sub, first = threads[thread]
        first += sum(len(step) for step in steps[:number])
        made = []
        for m, (s, hop, sent_off, arrive_off) in enumerate(steps[number]):
            dim = ORDERS[ch][s]
            n = dims[dim]
            index = lax.rem(pos[dim] + (arrive_off if arriving else sent_off) + n, n)
            piece = block(ch, s, index, sub)
            made.append(
                pltpu.make_async_remote_copy(
                    piece, piece, send.at[ch, first + m], recv.at[ch, first + m],
                    device_id=shifted(dim, hop), device_id_type=MESH_ID,
                )
            )
        return made

    sent, flying = [], {}

    def tick(ch, sub, number):
        thread = (ch, sub)
        steps = threads[thread][0]
        arrived = copies(thread, number - 1, True) if number else []
        leaving = copies(thread, number, False) if number < len(steps) else []
        paired = arrived and leaving and steps[number][0][0] == steps[number - 1][0][0]
        if paired and TWO not in KINDS[ch] and len(arrived) == len(leaving):
            for one, two in zip(arrived, leaving):
                one.wait_recv()
                two.start()
        else:
            for one in arrived:
                one.wait_recv()
            for two in leaving:
                two.start()
        for one in flying.pop(thread, ()):
            one.wait_send()
        flying[thread] = leaving

    def project(pair, i, dst):
        ch = 2 * pair
        last = {ORDERS[ch][2], ORDERS[ch + 1][2]}
        if last == {"x"}:
            at = lax.rem(x + (0, 1, 3, 2)[i], 4)
            b = [w[ch + e, :, at].reshape(1024, HEAD) for e in range(2)]
            a = [tok[:, :, pl.ds(pl.multiple_of(k * 1024 + at * 256, 256), 256)] for k in range(4)]
            a = jnp.concatenate(a, axis=2)
        else:
            at = lax.rem(y + (0, 1, 3, 2)[i], 4) if last == {"y"} else i
            b = [w[ch + e, at].reshape(1024, HEAD) for e in range(2)]
            a = tok[:, :, pl.ds(pl.multiple_of(at * 1024, 1024), 1024)]
        a = a.reshape(2 * SEG, 1024)
        b = jnp.concatenate(b, axis=1)
        r = jnp.dot(a, b, preferred_element_type=F32)
        if i:
            r += acc[pair]
        if i < 3:
            acc[pair] = r
        else:
            dst[...] = r.astype(BF16).reshape(2, SEG, CW)

    def delta():
        jrow = lax.broadcasted_iota(jnp.int32, (SEG, HEAD), 0)
        for g in range(2):
            cols = slice(g * HEAD, (g + 1) * HEAD)
            both = []
            for s in range(2):
                live = jrow < meta[s, 0:1, :]
                sig = jnp.where(live, sigma(kbuf[s, :, cols].astype(F32)), 0.0)
                zrow = jnp.sum(sig, axis=0, keepdims=True)
                m = lax.dot_general(
                    sig.astype(BF16), vbuf[s, :, cols], (((0,), (0,)), ((), ())), preferred_element_type=F32
                )
                both.append((m, zrow))
            own[g, 0:HEAD, :] = both[0][0]
            own[g, HEAD : HEAD + 16, :] = jnp.broadcast_to(both[0][1], (16, HEAD))
            rx[x, g, 0:HEAD, :] = (both[0][0] + both[1][0]).astype(BF16)
            rx[x, g, HEAD : HEAD + 16, :] = jnp.broadcast_to(both[0][1] + both[1][1], (16, HEAD)).astype(BF16)

    def exchange(dim, buf, number, arriving):
        n = dims[dim]
        copies = []
        for k in range(1, n):
            index = lax.rem(pos[dim] - k + n, n) if arriving else pos[dim]
            copies.append(
                pltpu.make_async_remote_copy(
                    buf.at[index], buf.at[index], dsem_s.at[number, k - 1], dsem_r.at[number, k - 1],
                    device_id=shifted(dim, k), device_id_type=MESH_ID,
                )
            )
        return copies

    def launch(copies):
        for one in copies:
            one.start()
        sent.extend(copies)

    def row_totals():
        for one in exchange("x", rx, 0, True):
            one.wait_recv()
        for g in range(2):
            total = jnp.zeros((HEAD + 16, HEAD), F32)
            for k in range(dims["x"]):
                total = total + rx[k, g].astype(F32)
            ry[y, g] = total.astype(BF16)
        launch(exchange("y", ry, 1, False))

    def memory():
        for one in exchange("y", ry, 1, True):
            one.wait_recv()
        for g in range(2):
            total = jnp.zeros((HEAD + 16, HEAD), F32)
            for k in range(dims["x"]):
                total = total + jnp.where(k < x, rx[k, g].astype(F32), 0.0)
            for k in range(dims["y"]):
                total = total + jnp.where(k < y, ry[k, g].astype(F32), 0.0)
            for s in range(2):
                if s:
                    total = total + own[g]
                mem[s, g, :, 0:HEAD] = total[0:HEAD].astype(BF16)
                zcol = jnp.transpose(jnp.broadcast_to(total[HEAD : HEAD + 1], (HEAD, HEAD)))
                mem[s, g, :, HEAD:] = zcol.astype(BF16)

    ones = jnp.ones((SEG, HEAD), BF16)

    def sides(j):
        return [jax.nn.sigmoid(jnp.full((1, HEAD), gate_ref[c * 8 + 2 * j + e], F32)) for e in range(2)]

    def stacked(j, s, rows):
        return jnp.concatenate([qbuf[j, s, rows, 0:HEAD], qbuf[j, s, rows, HEAD:]], axis=0)

    def attend(j, segments):
        kcols = slice(j // 2 * HEAD, (j // 2 + 1) * HEAD)
        gates = sides(j)
        blocks = [(s, r, (r + 1) * HEAD, slice(r * HEAD, (r + 1) * HEAD)) for r in (1, 0) for s in segments]
        scores = [
            lax.dot_general(
                stacked(j, s, rows), kbuf[s, 0:nk, kcols], (((1,), (1,)), ((), ())), preferred_element_type=F32
            )
            for s, r, nk, rows in blocks
        ]
        expo = []
        for (s, r, nk, rows), score in zip(blocks, scores):
            valid = meta[s, 0:1, :]
            irow = lax.broadcasted_iota(jnp.int32, (HEAD, nk), 0) + r * HEAD
            jcol = lax.broadcasted_iota(jnp.int32, (HEAD, nk), 1)
            wide = valid if r == 0 else jnp.concatenate([valid, valid], axis=1)
            allowed = (jcol <= irow) & (jcol < wide)
            if r:
                lower = jnp.concatenate([meta[s, 1:2, :], jnp.ones((1, HEAD), jnp.int32)], axis=1)
                allowed = allowed & (lower > 0)
            allowed = jnp.concatenate([allowed, allowed], axis=0)
            masked = jnp.where(allowed, score, -1e30)
            top = jnp.max(masked, axis=1, keepdims=True)
            expo.append(jnp.exp2((masked - top) * (HEAD**-0.5 * LOG2E)).astype(BF16))
        local = [
            jnp.dot(
                weights, jnp.concatenate([vbuf[s, 0:nk, kcols], ones[0:nk]], axis=1), preferred_element_type=F32
            )
            for (s, r, nk, rows), weights in zip(blocks, expo)
        ]
        for (s, r, nk, rows), one in zip(blocks, local):
            one = one[:, 0:HEAD] / jnp.maximum(one[:, HEAD:], 1.0)
            for e in range(2):
                half = slice(e * HEAD, (e + 1) * HEAD)
                loc[j, s, rows, half] = (1.0 - gates[e]) * one[half]

    def finish(j, second):
        s = c if second else 1 - c
        gates = sides(j)
        valid = meta[s, 0:1, :]
        first = pl.multiple_of(c * 4 * CW + j * CW, CW)
        for r in range(2):
            rows = slice(r * HEAD, (r + 1) * HEAD)
            sq = sigma(stacked(j, s, rows).astype(F32)).astype(BF16)
            retrieved = jnp.dot(sq, mem[s, j // 2], preferred_element_type=F32)
            remembered = retrieved[:, 0:HEAD] / (retrieved[:, HEAD:] + 1.0)
            alive = (lax.broadcasted_iota(jnp.int32, (HEAD, HEAD), 0) + r * HEAD) < valid
            for e in range(2):
                half = slice(e * HEAD, (e + 1) * HEAD)
                mixed = gates[e] * remembered[half] + loc[j, s, rows, half]
                mixed = jnp.where(alive, mixed, 0.0).astype(BF16)
                if second:
                    out_ref[rows, pl.ds(first + e * HEAD, HEAD)] = mixed
                else:
                    stage[j, rows, half] = mixed
        if not second:
            one = pltpu.make_async_remote_copy(
                stage.at[j], out_ref.at[:, pl.ds(first, CW)], osem_s.at[j], osem_r.at[j],
                device_id=sibling, device_id_type=MESH_ID,
            )
            one.start()
            sent.append(one)

    settled = set()

    def settle(ch):
        span = min(ch // 2, 2)
        if span not in settled:
            settled.add(span)
            locals_[span].wait()
            recvs_[span].wait_recv()
        w[ch, y, x, :, z] = wst[:, :, ch * HEAD : (ch + 1) * HEAD]

    last_pair = [where[0] for name, *where in PROGRAM if name == "local"][-1]
    for turn, (name, *where) in enumerate(PROGRAM):
        if turn == 24:
            meta_copy.start()
            tok_copy.start()
            tok_here.start()
        if name == "keys":
            if where[0] == 0:
                tok_here.wait()
                tok_back.wait_recv()
            project(0, where[0], kbuf)
        elif name == "values":
            project(1, where[0], vbuf)
        elif name == "q":
            project(2 + where[0], where[1], qbuf.at[where[0]])
        elif name == "delta":
            meta_back.wait_recv()
            delta()
            launch(exchange("x", rx, 0, False))
        elif name == "rows":
            row_totals()
        elif name == "memory":
            memory()
        elif name == "local":
            attend(where[0], (1 - c,) if where[0] == last_pair else (0, 1))
        elif name == "finish":
            finish(where[0], False)
            if where[0] != last_pair:
                finish(where[0], True)
        else:
            if where == [None, 0]:
                settle(name)
            tick(name, *where)

    attend(last_pair, (c,))
    finish(last_pair, True)

    for j in range(4):
        arriving = out_ref.at[:, pl.ds(pl.multiple_of((1 - c) * 4 * CW + j * CW, CW), CW)]
        pltpu.make_async_remote_copy(
            stage.at[j], arriving, osem_s.at[j], osem_r.at[j], device_id=sibling, device_id_type=MESH_ID
        ).wait_recv()
    for one in sent + sends_ + [meta_copy, tok_copy]:
        one.wait_send()


def solution(mesh):
    segs, nz = mesh.shape["seg"], mesh.shape["fsdp"]
    side = {32: 4, 8: 2, 16: 4}[segs]
    dims = {"x": side, "y": segs // 2 // side, "z": nz}

    def shards(tokens, w_query, w_key, value_weight, gate_bias, block_mask, valid_len):
        hbm = pl.BlockSpec(memory_space=pltpu.HBM)
        smem = pl.BlockSpec(memory_space=pltpu.SMEM)
        x, y, nz = dims["x"], dims["y"], dims["z"]
        dma = pltpu.SemaphoreType.DMA
        out = pl.pallas_call(
            functools.partial(body, dims),
            out_shape=pltpu.VMEM((SEG, 2048), BF16),
            in_specs=[hbm] * 4 + [smem] * 3,
            out_specs=pl.BlockSpec(memory_space=pltpu.VMEM),
            scratch_shapes=[
                pltpu.VMEM((2, 16, NCH * HEAD), BF16),
                pltpu.VMEM((NCH, y, x, 2, nz, 16, HEAD), BF16),
                pltpu.VMEM((2, SEG, 4096), BF16),
                pltpu.VMEM((6, 2 * SEG, CW), F32),
                pltpu.VMEM((2, SEG, CW), BF16),
                pltpu.VMEM((2, SEG, CW), BF16),
                pltpu.VMEM((4, 2, SEG, CW), BF16),
                pltpu.VMEM((2, 8, HEAD), jnp.int32),
                pltpu.VMEM((2, HEAD + 16, HEAD), F32),
                pltpu.VMEM((x, 2, HEAD + 16, HEAD), BF16),
                pltpu.VMEM((y, 2, HEAD + 16, HEAD), BF16),
                pltpu.VMEM((2, 2, HEAD, 2 * HEAD), BF16),
                pltpu.VMEM((4, 2, SEG, CW), F32),
                pltpu.VMEM((4, SEG, CW), BF16),
                dma((NCH, 20)),
                dma((NCH, 20)),
                dma((4,)),
                dma((5,)),
                dma((5,)),
                dma((2, 3)),
                dma((2, 3)),
                dma((4,)),
                dma((4,)),
            ],
            compiler_params=pltpu.CompilerParams(
                collective_id=0, has_side_effects=True, vmem_limit_bytes=56 * 1024 * 1024
            ),
        )(tokens[0], w_query, w_key, value_weight, gate_bias, block_mask[0, 0], valid_len)
        return out[None]

    in_specs = (
        P("fsdp", "seg", None),
        P(("seg", "fsdp"), None),
        P(("seg", "fsdp"), None),
        P(("seg", "fsdp"), None),
        P(),
        P("fsdp", "seg", None, None),
        P("fsdp", "seg"),
    )
    return jax.shard_map(
        shards, mesh=mesh, in_specs=in_specs, out_specs=P("fsdp", "seg", None), check_vma=False
    )
```

```python
import functools

import jax
import jax.numpy as jnp
from jax import lax
from jax.experimental import pallas as pl
from jax.experimental.pallas import tpu as pltpu
from jax.sharding import PartitionSpec as P

HEAD = 128
SEG = 256
CW = 256
NCH = 12
DIRECT, TWO, RING = "direct", "two", "ring"
ORDERS = ("zyx", "zxy", "xyz", "xyz", "zyx", "zxy", "yxz", "xyz", "zyx", "zyx", "zxy", "zxy")
KINDS = (
    (DIRECT, DIRECT, 2, 0), (DIRECT, DIRECT, 2, 0), (DIRECT, DIRECT, 1, 1),
    (DIRECT, RING, 1, 0), (TWO, RING, 2, 1), (TWO, RING, 2, 1),
    (DIRECT, RING, 1, 0), (DIRECT, DIRECT, 1, 1), (RING, RING, 2, 0),
    (TWO, RING, 2, 1), (RING, RING, 2, 0), (TWO, RING, 2, 1),
)
MESH_ID = pl.DeviceIdType.MESH
F32 = jnp.float32
LOG2E = 1.4426950408889634
BF16 = jnp.bfloat16

PROGRAM = (
    (3, None, 0), (0, None, 0), (1, None, 0), (2, None, 0), (4, None, 0), (5, None, 0), (6, None, 0), (8, None, 0),
    (10, None, 0), (3, None, 1), (2, None, 1), (9, None, 0), (11, None, 0), (7, None, 0), (0, None, 1),
    (6, None, 1), (1, None, 1), (3, None, 2), (4, None, 1), (5, None, 1), (8, None, 1), (10, None, 1), (7, None, 1),
    (2, None, 2), (2, 0, 0), (9, None, 1), (6, None, 2), (11, None, 1), (4, None, 2), (5, None, 2), (8, None, 2),
    (10, None, 2), (0, None, 2), (0, 0, 0), (0, 1, 0), (3, None, 3), (3, 0, 0), (1, None, 2), (1, 0, 0), (1, 1, 0),
    (6, None, 3), (7, None, 2), (2, 0, 1), (9, None, 2), (5, None, 3), (4, None, 3), (11, None, 2), (8, None, 3),
    (10, None, 3), (0, 0, 1), (1, 0, 1), (3, 0, 1), (0, 1, 1), (8, None, 4), (10, None, 4), (1, 1, 1), (2, 0, 2),
    (5, None, 4), (5, 0, 0), (5, 1, 0), (9, None, 3), (4, None, 4), (4, 0, 0), (4, 1, 0), (11, None, 3), (3, 0, 2),
    (0, 0, 2), (1, 0, 2), (0, 1, 2), (8, None, 5), (2, 0, 3), (6, 0, 0), (1, 1, 2), ("keys", 0), (10, None, 5),
    ("keys", 1), ("keys", 2), ("keys", 3), (3, 0, 3), (7, 0, 0), (5, 0, 1), (4, 0, 1), (2, 0, 4), (10, None, 6),
    (10, 0, 0), (4, 1, 1), (5, 1, 1), (10, 1, 0), (8, None, 6), (8, 0, 0), (8, 1, 0), (9, None, 4), (9, 0, 0),
    (11, None, 4), (11, 0, 0), (3, 0, 4), ("values", 0), ("values", 1), (6, 0, 1), ("values", 2), ("values", 3),
    (4, 0, 2), ("delta",), (5, 0, 2), (7, 0, 1), (4, 1, 2), (10, 0, 1), (11, 1, 0), ("q", 3, 0), (6, 0, 2),
    (5, 1, 2), ("q", 0, 0), (8, 0, 1), (9, 1, 0), ("q", 0, 1), ("q", 0, 2), ("q", 0, 3), ("q", 2, 0), ("local", 0),
    (10, 1, 1), (8, 1, 1), (7, 0, 2), (6, 0, 3), (11, 0, 1), (9, 0, 1), (10, 0, 2), (7, 0, 3), (8, 0, 2),
    (11, 1, 1), ("q", 3, 1), ("q", 3, 2), ("rows",), (6, 0, 4), (10, 1, 2), (9, 1, 1), ("q", 2, 1), (11, 0, 2),
    ("q", 2, 2), (7, 0, 4), ("q", 1, 0), ("q", 1, 1), ("q", 1, 2), ("q", 1, 3), (8, 1, 2), (11, 1, 2), ("q", 3, 3),
    (9, 0, 2), ("local", 1), ("local", 3), (9, 1, 2), ("q", 2, 3), ("local", 2), ("memory",), ("finish", 0),
    ("finish", 1), ("finish", 2), ("finish", 3),
)


def sigma(v):
    return jnp.where(v > 0, v, jnp.exp(jnp.minimum(v, 0.0)) - 1.0) + 1.0


def body(
    dims,
    tok_hbm, wq_hbm, wk_hbm, wv_hbm, gate_ref, mask_ref, valid_ref,
    out_ref,
    wst, w, tok, acc, kbuf, vbuf, qbuf, meta, own, rx, ry, mem, loc, stage,
    recv, send, csem_l, csem_s, csem_r, dsem_s, dsem_r, osem_s, osem_r,
):
    seg = lax.axis_index("seg")
    z = lax.axis_index("fsdp")
    c = lax.rem(seg, 2)
    x = lax.rem(seg // 2, dims["x"])
    y = seg // (2 * dims["x"])
    pos = {"x": x, "y": y, "z": z}

    def device(xx, yy, cc, zz):
        return {"seg": (yy * dims["x"] + xx) * 2 + cc, "fsdp": zz}

    def shifted(dim, delta):
        at = dict(pos)
        at[dim] = lax.rem(pos[dim] + delta + dims[dim], dims[dim])
        return device(at["x"], at["y"], c, at["z"])

    sibling = device(x, y, 1 - c, z)

    barrier = pltpu.get_barrier_semaphore()
    peers = [sibling]
    for dim in "xyz":
        peers += [shifted(dim, k) for k in range(1, dims[dim])]
    for peer in peers:
        pl.semaphore_signal(barrier, inc=1, device_id=peer, device_id_type=MESH_ID)
    pl.semaphore_wait(barrier, len(peers))

    def columns(core):
        wide = pl.ds(pl.multiple_of(core * CW, CW), CW)
        return (wk_hbm.at[:, wide], wv_hbm.at[:, wide], wq_hbm.at[:, pl.ds(pl.multiple_of(core * 4 * CW, CW), 4 * CW)])

    spans = (slice(0, CW), slice(CW, 2 * CW), slice(2 * CW, 6 * CW))
    locals_, sends_, recvs_ = [], [], []
    for i, span in enumerate(spans):
        there = pltpu.make_async_remote_copy(
            columns(1 - c)[i], wst.at[c, :, span], csem_s.at[i], csem_r.at[i],
            device_id=sibling, device_id_type=MESH_ID,
        )
        there.start()
        here = pltpu.make_async_copy(columns(c)[i], wst.at[c, :, span], csem_l.at[i])
        here.start()
        other = wst.at[1 - c, :, span]
        back = pltpu.make_async_remote_copy(
            other, other, csem_s.at[i], csem_r.at[i], device_id=sibling, device_id_type=MESH_ID
        )
        locals_.append(here)
        sends_.append(there)
        recvs_.append(back)

    row8 = lax.broadcasted_iota(jnp.int32, (8, HEAD), 0)
    meta[c] = jnp.where(row8 == 0, valid_ref[0], mask_ref[1, 0])
    meta_copy = pltpu.make_async_remote_copy(
        meta.at[c], meta.at[c], csem_s.at[3], csem_r.at[3], device_id=sibling, device_id_type=MESH_ID
    )
    meta_back = pltpu.make_async_remote_copy(
        meta.at[1 - c], meta.at[1 - c], csem_s.at[3], csem_r.at[3], device_id=sibling, device_id_type=MESH_ID
    )
    tok_copy = pltpu.make_async_remote_copy(
        tok_hbm, tok.at[c], csem_s.at[4], csem_r.at[4], device_id=sibling, device_id_type=MESH_ID
    )
    tok_back = pltpu.make_async_remote_copy(
        tok.at[1 - c], tok.at[1 - c], csem_s.at[4], csem_r.at[4], device_id=sibling, device_id_type=MESH_ID
    )
    tok_here = pltpu.make_async_copy(tok_hbm, tok.at[c], csem_l.at[3])

    def block(ch, stage_no, index, sub):
        order = ORDERS[ch]
        at = {d: pl.ds(pos[d], 1) for d in "xyz"}
        for d in order[:stage_no]:
            at[d] = slice(None)
        at[order[stage_no]] = pl.ds(index, 1)
        cores = slice(None) if sub is None else pl.ds(sub, 1)
        return w.at[ch, at["y"], at["x"], cores, at["z"]]

    def stage_steps(ch, s, kind, even):
        n = dims[ORDERS[ch][s]]
        if kind == DIRECT:
            return [[(s, k, 0, -k) for k in range(1, n)]]
        if kind == TWO and n == 8:
            far = (s, 2, -2, -4) if even else (s, -2, 2, 4)
            return [
                [(s, 1, 0, -1), (s, -1, 0, 1), (s, 2, 0, -2), (s, -2, 0, 2)],
                [(s, -1, 2, 3), (s, 1, -2, -3), far],
            ]
        made = []
        for k in range(1, n // 2 + 1):
            sides = (1, -1) if 2 * k < n else ((1,) if even else (-1,))
            made.append([(s, side, -side * (k - 1), -side * k) for side in sides])
        return made

    threads = {}
    for ch in range(NCH):
        k1, k2, subs, odd = KINDS[ch]
        even = not odd
        steps = stage_steps(ch, 0, k1, even) + stage_steps(ch, 1, k2, even)
        threads[ch, None] = (steps, None, 0)
        used = sum(len(step) for step in steps)
        for h in range(subs):
            steps = stage_steps(ch, 2, RING, h == 0 if subs == 2 else even)
            threads[ch, h] = (steps, h if subs == 2 else None, used)
            used += sum(len(step) for step in steps)

    def copies(thread, number, arriving):
        ch = thread[0]
        steps, sub, first = threads[thread]
        first += sum(len(step) for step in steps[:number])
        made = []
        for m, (s, hop, sent_off, arrive_off) in enumerate(steps[number]):
            dim = ORDERS[ch][s]
            n = dims[dim]
            index = lax.rem(pos[dim] + (arrive_off if arriving else sent_off) + n, n)
            piece = block(ch, s, index, sub)
            made.append(
                pltpu.make_async_remote_copy(
                    piece, piece, send.at[ch, first + m], recv.at[ch, first + m],
                    device_id=shifted(dim, hop), device_id_type=MESH_ID,
                )
            )
        return made

    sent, flying = [], {}

    def tick(ch, sub, number):
        thread = (ch, sub)
        steps = threads[thread][0]
        arrived = copies(thread, number - 1, True) if number else []
        leaving = copies(thread, number, False) if number < len(steps) else []
        paired = arrived and leaving and steps[number][0][0] == steps[number - 1][0][0]
        if paired and TWO not in KINDS[ch] and len(arrived) == len(leaving):
            for one, two in zip(arrived, leaving):
                one.wait_recv()
                two.start()
        else:
            for one in arrived:
                one.wait_recv()
            for two in leaving:
                two.start()
        for one in flying.pop(thread, ()):
            one.wait_send()
        flying[thread] = leaving

    def project(pair, i, dst):
        ch = 2 * pair
        last = {ORDERS[ch][2], ORDERS[ch + 1][2]}
        if last == {"x"}:
            at = lax.rem(x + (0, 1, 3, 2)[i], 4)
            b = [w[ch + e, :, at].reshape(1024, HEAD) for e in range(2)]
            a = [tok[:, :, pl.ds(pl.multiple_of(k * 1024 + at * 256, 256), 256)] for k in range(4)]
            a = jnp.concatenate(a, axis=2)
        else:
            at = lax.rem(y + (0, 1, 3, 2)[i], 4) if last == {"y"} else i
            b = [w[ch + e, at].reshape(1024, HEAD) for e in range(2)]
            a = tok[:, :, pl.ds(pl.multiple_of(at * 1024, 1024), 1024)]
        a = a.reshape(2 * SEG, 1024)
        b = jnp.concatenate(b, axis=1)
        r = jnp.dot(a, b, preferred_element_type=F32)
        if i:
            r += acc[pair]
        if i < 3:
            acc[pair] = r
        else:
            dst[...] = r.astype(BF16).reshape(2, SEG, CW)

    def delta():
        jrow = lax.broadcasted_iota(jnp.int32, (SEG, HEAD), 0)
        for g in range(2):
            cols = slice(g * HEAD, (g + 1) * HEAD)
            both = []
            for s in range(2):
                live = jrow < meta[s, 0:1, :]
                sig = jnp.where(live, sigma(kbuf[s, :, cols].astype(F32)), 0.0)
                zrow = jnp.sum(sig, axis=0, keepdims=True)
                m = lax.dot_general(
                    sig.astype(BF16), vbuf[s, :, cols], (((0,), (0,)), ((), ())), preferred_element_type=F32
                )
                both.append((m, zrow))
            own[g, 0:HEAD, :] = both[0][0]
            own[g, HEAD : HEAD + 16, :] = jnp.broadcast_to(both[0][1], (16, HEAD))
            rx[x, g, 0:HEAD, :] = (both[0][0] + both[1][0]).astype(BF16)
            rx[x, g, HEAD : HEAD + 16, :] = jnp.broadcast_to(both[0][1] + both[1][1], (16, HEAD)).astype(BF16)

    def exchange(dim, buf, number, arriving):
        n = dims[dim]
        copies = []
        for k in range(1, n):
            index = lax.rem(pos[dim] - k + n, n) if arriving else pos[dim]
            copies.append(
                pltpu.make_async_remote_copy(
                    buf.at[index], buf.at[index], dsem_s.at[number, k - 1], dsem_r.at[number, k - 1],
                    device_id=shifted(dim, k), device_id_type=MESH_ID,
                )
            )
        return copies

    def launch(copies):
        for one in copies:
            one.start()
        sent.extend(copies)

    def row_totals():
        for one in exchange("x", rx, 0, True):
            one.wait_recv()
        for g in range(2):
            total = jnp.zeros((HEAD + 16, HEAD), F32)
            for k in range(dims["x"]):
                total = total + rx[k, g].astype(F32)
            ry[y, g] = total.astype(BF16)
        launch(exchange("y", ry, 1, False))

    def memory():
        for one in exchange("y", ry, 1, True):
            one.wait_recv()
        for g in range(2):
            total = jnp.zeros((HEAD + 16, HEAD), F32)
            for k in range(dims["x"]):
                total = total + jnp.where(k < x, rx[k, g].astype(F32), 0.0)
            for k in range(dims["y"]):
                total = total + jnp.where(k < y, ry[k, g].astype(F32), 0.0)
            for s in range(2):
                if s:
                    total = total + own[g]
                mem[s, g, :, 0:HEAD] = total[0:HEAD].astype(BF16)
                zcol = jnp.transpose(jnp.broadcast_to(total[HEAD : HEAD + 1], (HEAD, HEAD)))
                mem[s, g, :, HEAD:] = zcol.astype(BF16)

    ones = jnp.ones((SEG, HEAD), BF16)

    def sides(j):
        return [jax.nn.sigmoid(jnp.full((1, HEAD), gate_ref[c * 8 + 2 * j + e], F32)) for e in range(2)]

    def stacked(j, s, rows):
        return jnp.concatenate([qbuf[j, s, rows, 0:HEAD], qbuf[j, s, rows, HEAD:]], axis=0)

    def attend(j, segments):
        kcols = slice(j // 2 * HEAD, (j // 2 + 1) * HEAD)
        gates = sides(j)
        blocks = [(s, r, (r + 1) * HEAD, slice(r * HEAD, (r + 1) * HEAD)) for r in (1, 0) for s in segments]
        scores = [
            lax.dot_general(
                stacked(j, s, rows), kbuf[s, 0:nk, kcols], (((1,), (1,)), ((), ())), preferred_element_type=F32
            )
            for s, r, nk, rows in blocks
        ]
        expo = []
        for (s, r, nk, rows), score in zip(blocks, scores):
            valid = meta[s, 0:1, :]
            irow = lax.broadcasted_iota(jnp.int32, (HEAD, nk), 0) + r * HEAD
            jcol = lax.broadcasted_iota(jnp.int32, (HEAD, nk), 1)
            wide = valid if r == 0 else jnp.concatenate([valid, valid], axis=1)
            allowed = (jcol <= irow) & (jcol < wide)
            if r:
                lower = jnp.concatenate([meta[s, 1:2, :], jnp.ones((1, HEAD), jnp.int32)], axis=1)
                allowed = allowed & (lower > 0)
            allowed = jnp.concatenate([allowed, allowed], axis=0)
            masked = jnp.where(allowed, score, -1e30)
            top = jnp.max(masked, axis=1, keepdims=True)
            expo.append(jnp.exp2((masked - top) * (HEAD**-0.5 * LOG2E)).astype(BF16))
        local = [
            jnp.dot(
                weights, jnp.concatenate([vbuf[s, 0:nk, kcols], ones[0:nk]], axis=1), preferred_element_type=F32
            )
            for (s, r, nk, rows), weights in zip(blocks, expo)
        ]
        for (s, r, nk, rows), one in zip(blocks, local):
            one = one[:, 0:HEAD] / jnp.maximum(one[:, HEAD:], 1.0)
            for e in range(2):
                half = slice(e * HEAD, (e + 1) * HEAD)
                loc[j, s, rows, half] = (1.0 - gates[e]) * one[half]

    def finish(j, second):
        s = c if second else 1 - c
        gates = sides(j)
        valid = meta[s, 0:1, :]
        first = pl.multiple_of(c * 4 * CW + j * CW, CW)
        for r in range(2):
            rows = slice(r * HEAD, (r + 1) * HEAD)
            sq = sigma(stacked(j, s, rows).astype(F32)).astype(BF16)
            retrieved = jnp.dot(sq, mem[s, j // 2], preferred_element_type=F32)
            remembered = retrieved[:, 0:HEAD] / (retrieved[:, HEAD:] + 1.0)
            alive = (lax.broadcasted_iota(jnp.int32, (HEAD, HEAD), 0) + r * HEAD) < valid
            for e in range(2):
                half = slice(e * HEAD, (e + 1) * HEAD)
                mixed = gates[e] * remembered[half] + loc[j, s, rows, half]
                mixed = jnp.where(alive, mixed, 0.0).astype(BF16)
                if second:
                    out_ref[rows, pl.ds(first + e * HEAD, HEAD)] = mixed
                else:
                    stage[j, rows, half] = mixed
        if not second:
            one = pltpu.make_async_remote_copy(
                stage.at[j], out_ref.at[:, pl.ds(first, CW)], osem_s.at[j], osem_r.at[j],
                device_id=sibling, device_id_type=MESH_ID,
            )
            one.start()
            sent.append(one)

    settled = set()

    def settle(ch):
        span = min(ch // 2, 2)
        if span not in settled:
            settled.add(span)
            locals_[span].wait()
            recvs_[span].wait_recv()
        w[ch, y, x, :, z] = wst[:, :, ch * HEAD : (ch + 1) * HEAD]

    last_pair = [where[0] for name, *where in PROGRAM if name == "local"][-1]
    for turn, (name, *where) in enumerate(PROGRAM):
        if turn == 24:
            meta_copy.start()
            tok_copy.start()
            tok_here.start()
        if name == "keys":
            if where[0] == 0:
                tok_here.wait()
                tok_back.wait_recv()
            project(0, where[0], kbuf)
        elif name == "values":
            project(1, where[0], vbuf)
        elif name == "q":
            project(2 + where[0], where[1], qbuf.at[where[0]])
        elif name == "delta":
            meta_back.wait_recv()
            delta()
            launch(exchange("x", rx, 0, False))
        elif name == "rows":
            row_totals()
        elif name == "memory":
            memory()
        elif name == "local":
            attend(where[0], (1 - c,) if where[0] == last_pair else (0, 1))
        elif name == "finish":
            finish(where[0], False)
            if where[0] != last_pair:
                finish(where[0], True)
        else:
            if where == [None, 0]:
                settle(name)
            tick(name, *where)

    attend(last_pair, (c,))
    finish(last_pair, True)

    for j in range(4):
        arriving = out_ref.at[:, pl.ds(pl.multiple_of((1 - c) * 4 * CW + j * CW, CW), CW)]
        pltpu.make_async_remote_copy(
            stage.at[j], arriving, osem_s.at[j], osem_r.at[j], device_id=sibling, device_id_type=MESH_ID
        ).wait_recv()
    for one in sent + sends_ + [meta_copy, tok_copy]:
        one.wait_send()


def solution(mesh):
    segs, nz = mesh.shape["seg"], mesh.shape["fsdp"]
    side = {32: 4, 8: 2, 16: 4}[segs]
    dims = {"x": side, "y": segs // 2 // side, "z": nz}

    def shards(tokens, w_query, w_key, value_weight, gate_bias, block_mask, valid_len):
        hbm = pl.BlockSpec(memory_space=pltpu.HBM)
        smem = pl.BlockSpec(memory_space=pltpu.SMEM)
        x, y, nz = dims["x"], dims["y"], dims["z"]
        dma = pltpu.SemaphoreType.DMA
        out = pl.pallas_call(
            functools.partial(body, dims),
            out_shape=pltpu.VMEM((SEG, 2048), BF16),
            in_specs=[hbm] * 4 + [smem] * 3,
            out_specs=pl.BlockSpec(memory_space=pltpu.VMEM),
            scratch_shapes=[
                pltpu.VMEM((2, 16, NCH * HEAD), BF16),
                pltpu.VMEM((NCH, y, x, 2, nz, 16, HEAD), BF16),
                pltpu.VMEM((2, SEG, 4096), BF16),
                pltpu.VMEM((6, 2 * SEG, CW), F32),
                pltpu.VMEM((2, SEG, CW), BF16),
                pltpu.VMEM((2, SEG, CW), BF16),
                pltpu.VMEM((4, 2, SEG, CW), BF16),
                pltpu.VMEM((2, 8, HEAD), jnp.int32),
                pltpu.VMEM((2, HEAD + 16, HEAD), F32),
                pltpu.VMEM((x, 2, HEAD + 16, HEAD), BF16),
                pltpu.VMEM((y, 2, HEAD + 16, HEAD), BF16),
                pltpu.VMEM((2, 2, HEAD, 2 * HEAD), BF16),
                pltpu.VMEM((4, 2, SEG, CW), F32),
                pltpu.VMEM((4, SEG, CW), BF16),
                dma((NCH, 20)),
                dma((NCH, 20)),
                dma((4,)),
                dma((5,)),
                dma((5,)),
                dma((2, 3)),
                dma((2, 3)),
                dma((4,)),
                dma((4,)),
            ],
            compiler_params=pltpu.CompilerParams(
                collective_id=0, has_side_effects=True, vmem_limit_bytes=56 * 1024 * 1024
            ),
        )(tokens[0], w_query, w_key, value_weight, gate_bias, block_mask[0, 0], valid_len.reshape(1))
        return out[None]

    in_specs = (
        P("fsdp", "seg", None),
        P(("seg", "fsdp"), None),
        P(("seg", "fsdp"), None),
        P(("seg", "fsdp"), None),
        P(),
        P("fsdp", "seg", None, None),
        P("fsdp", "seg"),
    )
    return jax.shard_map(
        shards, mesh=mesh, in_specs=in_specs, out_specs=P("fsdp", "seg", None), check_vma=False
    )
```
